32 devices in a mesh: shape: 8 (over z, x), cls: 4 (over y, core).
Axes of the slice: x: 2, y: 2, z: 4, core: 2. Of those that a mesh axis runs over, the one named last changes fastest.
Arguments:
- shapes: bfloat16 [4096, 1280], P('shape', 'cls'), may hold values from -600 to 600
- classes: bfloat16 [20480, 1280], P('cls'), may hold values from -400 to 400
- counts: int32 [20480], P('cls'), may hold values from 0 to 2, as said below
Outputs:
- assignment: bfloat16 [4096, 20480], P('shape', 'cls')
The draws below stay inside these ranges and needn't reach their ends.
Inputs may be any that keep to these rules, and one draw needn't show every extreme that they name: The counts sum to 4096; exactly 1024 classes have count 2.
All inputs are finite; a program needn't handle non-finite values.
Results may differ from the reference program's by a relative error of at most 0.001.
Values may be sent and summed in bfloat16 or wider, within the bound.
No kernel may reach another device: no remote copies, remote signals or barrier semaphores. Data moves between devices by JAX's collectives and lax.ppermute only.
A program may use at most 128 MiB of HBM per device.

```python
import math
import jax
import jax.numpy as jnp
from jax import lax

E = 1280
CLASSES = 20480
ITERS = 3
SHAPES = 4096


log_ten = math.log(10.0)


def unit_noise(key, rows):
    return jnp.clip(jax.random.normal(key, (rows, E), jnp.float32), -4.0, 4.0)


def feature_scales(key):
    return jnp.exp(log_ten * jax.random.uniform(jax.random.fold_in(key, 5), (E,), jnp.float32))


def class_base(key):
    return unit_noise(jax.random.fold_in(key, 11), CLASSES)


def draw_classes(key, part):
    row_scale = jnp.exp(log_ten * jax.random.uniform(jax.random.fold_in(key, 13), (CLASSES, 1), jnp.float32))
    values = feature_scales(key)[None, :] * class_base(key) * row_scale
    return values.astype(jnp.bfloat16)


def draw_shapes(key, part):
    prototype = jax.random.randint(jax.random.fold_in(key, 17), (SHAPES,), 0, CLASSES).astype(jnp.int32)
    mixing = jax.random.uniform(jax.random.fold_in(key, 19), (SHAPES, 1), jnp.float32, 0.15, 0.4)
    noise = unit_noise(jax.random.fold_in(key, 23), SHAPES)
    anchors = jnp.take(class_base(key), prototype, axis=0)
    mixed = mixing * anchors + jnp.sqrt(1.0 - mixing * mixing) * noise
    row_scale = jnp.exp(log_ten * jax.random.uniform(jax.random.fold_in(key, 31), (SHAPES, 1), jnp.float32))
    values = feature_scales(key)[None, :] * mixed * row_scale
    return values.astype(jnp.bfloat16)


def draw_counts(key, part):
    order = jax.random.permutation(jax.random.fold_in(key, 3), CLASSES).astype(jnp.int32)
    ranks = jnp.zeros((CLASSES,), jnp.int32).at[order].set(jnp.arange(CLASSES, dtype=jnp.int32))
    doubled = SHAPES // 4
    singles_end = SHAPES - doubled
    return jnp.where(ranks < doubled, 2, jnp.where(ranks < singles_end, 1, 0)).astype(jnp.int32)


def setup_inputs(seed: int = 0) -> dict:
    splits = jax.random.split(jax.random.key(seed), 4)
    return {
        "shapes": draw_shapes(jax.random.fold_in(splits[3], 71), 0),
        "classes": draw_classes(jax.random.fold_in(splits[3], 71), 0),
        "counts": draw_counts(jax.random.fold_in(splits[3], 71), 0),
    }


logit_scale = 40.0
epsilon = 1e-06

def reference(shapes, classes, counts):
    shape_f = shapes.astype(jnp.float32)
    class_f = classes.astype(jnp.float32)
    shape_scale = lax.rsqrt(lax.optimization_barrier(jnp.sum(shape_f * shape_f, axis=1)) + epsilon)
    class_scale = lax.rsqrt(lax.optimization_barrier(jnp.sum(class_f * class_f, axis=1)) + epsilon)
    products = jnp.dot(shape_f, class_f.T, precision=lax.Precision.HIGHEST)
    kernel = jnp.exp(logit_scale * products * shape_scale[:, None] * class_scale[None, :])
    target = counts.astype(jnp.float32)
    row_inv = 1.0 / lax.optimization_barrier(jnp.sum(kernel, axis=1))
    col_scale = jnp.zeros((CLASSES,), jnp.float32)
    for step in range(ITERS):
        col_scale = target / jnp.dot(row_inv, kernel, precision=lax.Precision.HIGHEST)
        row_inv = 1.0 / jnp.dot(kernel, col_scale, precision=lax.Precision.HIGHEST)
    result = row_inv[:, None] * kernel * col_scale[None, :]
    return result.astype(jnp.bfloat16)
```

```python
import jax
import jax.numpy as jnp
from jax import lax
from jax.sharding import PartitionSpec as P

ITERS = 3

logit_scale = 40.0
epsilon = 1e-06


def exchange(value, axis, bit):
    size = lax.axis_size(axis)
    return lax.ppermute(value, axis, [(i, i ^ bit) for i in range(size)])


def bits(axis):
    size = lax.axis_size(axis)
    assert size & (size - 1) == 0
    return [1 << b for b in range(size.bit_length() - 1)]


def total(value, axis):
    for bit in bits(axis):
        value = value + exchange(value, axis, bit)
    return value


def shards(shapes, classes, counts):
    n = lax.axis_size("cls")
    me = lax.axis_index("cls")
    held = [shapes.T]
    for bit in reversed(bits("cls")):
        held = held + [exchange(h, "cls", bit) for h in held]
    order = [0]
    for bit in reversed(bits("cls")):
        order = order + [o ^ bit for o in order]
    stacked = jnp.stack(held)
    where = {o: i for i, o in enumerate(order)}
    index = jnp.stack([jnp.array([where[k ^ m] for k in range(n)], jnp.int32) for m in range(n)])[me]
    piece = jnp.concatenate([lax.dynamic_index_in_dim(stacked, index[k], 0, keepdims=False) for k in range(n)])
    class_f = classes.astype(jnp.float32)
    class_scale = lax.rsqrt(jnp.sum(class_f * class_f, axis=1) + epsilon)
    term = lax.dot_general(
        piece, classes, (((0,), (1,)), ((), ())), preferred_element_type=jnp.float32
    )
    piece_f = piece.astype(jnp.float32)
    squares = jnp.sum(piece_f * piece_f, axis=0)
    shape_scale = lax.rsqrt(squares + epsilon)
    kernel = jnp.exp(logit_scale * term * shape_scale[:, None] * class_scale[None, :])
    target = counts.astype(jnp.float32)
    row_inv = 1.0 / total(jnp.sum(kernel, axis=1), "cls")
    col_scale = jnp.zeros((classes.shape[0],), jnp.float32)
    for step in range(ITERS):
        column_part = jnp.dot(row_inv, kernel, precision=lax.Precision.HIGHEST)
        col_scale = target / total(column_part, "shape")
        row_inv = 1.0 / total(jnp.dot(kernel, col_scale, precision=lax.Precision.HIGHEST), "cls")
    result = row_inv[:, None] * kernel * col_scale[None, :]
    return result.astype(jnp.bfloat16)


def solution(mesh):
    placed = (P("shape", "cls"), P("cls", None), P("cls"))
    return jax.shard_map(
        shards, mesh=mesh, in_specs=placed, out_specs=P("shape", "cls"), check_vma=False
    )
```

```python
import functools

import jax
import jax.numpy as jnp
from jax import lax
from jax.experimental import pallas as pl
from jax.experimental.pallas import tpu as pltpu
from jax.sharding import PartitionSpec as P

ITERS = 3

logit_scale = 40.0
epsilon = 1e-06
LANES = 128
VMEM = pltpu.VMEM
SMALL = pltpu.CompilerParams(vmem_limit_bytes=16 << 20)


def bits(axis):
    size = lax.axis_size(axis)
    assert size & (size - 1) == 0
    return [1 << b for b in range(size.bit_length() - 1)]


def exchange(value, axis, bit):
    size = lax.axis_size(axis)
    return lax.ppermute(value, axis, [(i, i ^ bit) for i in range(size)])


def halves(value, axis):
    steps = bits(axis)
    for bit in steps[:-1]:
        value = value + exchange(value, axis, bit)
    return value, exchange(value, axis, steps[-1])


def whole(count):
    return [pl.BlockSpec(memory_space=VMEM)] * count


def tile(index):
    return pl.ds(pl.multiple_of(index * LANES, LANES), LANES)


def to_lanes(value):
    return jnp.sum(value.T, axis=0, keepdims=True)


def to_rows(value):
    return jnp.broadcast_to(value, (LANES, value.shape[1])).T


def kernel_body(chunks, block, me_ref, *refs):
    piece_refs = refs[:chunks]
    scale_ref, classes_ref, kernel_ref, sums_ref, turned, lhs, held, factor, part, sems = refs[chunks:]
    rows = lhs.shape[0]
    blocks = held.shape[0]

    def fetch(i):
        return pltpu.make_async_copy(classes_ref.at[pl.ds(i * block, block), :], held.at[i], sems.at[i])

    for i in range(blocks):
        fetch(i).start()
    depth = piece_refs[0].shape[0]
    me = me_ref[0]
    for offset in range(chunks):
        at = pl.multiple_of(lax.bitwise_xor(me, offset) * depth, depth)
        turned[pl.ds(at, depth), :] = piece_refs[offset][...]
    lhs[...] = turned[...].T
    square = jnp.zeros((rows, LANES), jnp.float32)
    for t in range(lhs.shape[1] // LANES):
        value = lhs[:, t * LANES : (t + 1) * LANES].astype(jnp.float32)
        square = square + value * value
    inverse = logit_scale * lax.rsqrt(jnp.sum(square, axis=1, keepdims=True) + epsilon)
    factor[...] = jnp.broadcast_to(inverse, (rows, LANES))
    part[...] = jnp.zeros_like(part)

    def step(i, carry):
        fetch(i).wait()
        products = lax.dot_general(
            lhs[...], held[i], (((1,), (1,)), ((), ())), preferred_element_type=jnp.float32
        )
        total = part[...]
        for t in range(block // LANES):
            at = tile(i * (block // LANES) + t)
            value = products[:, t * LANES : (t + 1) * LANES]
            value = jnp.exp(value * factor[...] * scale_ref[:, at])
            kernel_ref[:, at] = value
            total = total + value
        part[...] = total
        return carry

    lax.fori_loop(0, blocks, step, 0)
    sums_ref[...] = to_lanes(part[...])


def make_kernel(me, pieces, class_scale, classes):
    count, width = classes.shape
    rows = pieces[0].shape[1]
    block = min(512, count)
    while count % block:
        block -= LANES
    blocks = count // block
    return pl.pallas_call(
        functools.partial(kernel_body, len(pieces), block),
        out_shape=(VMEM((rows, count), jnp.float32), VMEM((1, rows), jnp.float32)),
        in_specs=[pl.BlockSpec(memory_space=pltpu.SMEM)]
        + whole(len(pieces) + 1)
        + [pl.BlockSpec(memory_space=pl.ANY)],
        out_specs=tuple(whole(2)),
        scratch_shapes=[
            VMEM((width, rows), jnp.bfloat16),
            VMEM((rows, width), jnp.bfloat16),
            VMEM((blocks, block, width), jnp.bfloat16),
            VMEM((rows, LANES), jnp.float32),
            VMEM((rows, LANES), jnp.float32),
            pltpu.SemaphoreType.DMA((blocks,)),
        ],
        compiler_params=pltpu.CompilerParams(vmem_limit_bytes=44 << 20),
        name="make_kernel",
    )(me, *pieces, class_scale, classes)


def column_body(kernel_ref, near_ref, far_ref, out_ref, spread):
    spread[...] = to_rows(1.0 / (near_ref[...] + far_ref[...]))
    rows = spread.shape[0]

    def step(j, carry):
        value = kernel_ref[:, tile(j)] * spread[...]
        out_ref[:, tile(j)] = jnp.sum(value, axis=0, keepdims=True)
        return carry

    lax.fori_loop(0, kernel_ref.shape[1] // LANES, step, 0, unroll=4)


def column_sums(kernel, near, far):
    rows, count = kernel.shape
    return pl.pallas_call(
        column_body,
        out_shape=jax.ShapeDtypeStruct((1, count), jnp.float32),
        in_specs=whole(3),
        out_specs=whole(1)[0],
        scratch_shapes=[VMEM((rows, LANES), jnp.float32)],
        compiler_params=SMALL,
        name="column_sums",
    )(pltpu.with_memory_space_constraint(kernel, VMEM), near, far)


def row_body(kernel_ref, near_ref, far_ref, counts_ref, out_ref, scale_ref, part):
    scale_ref[...] = counts_ref[...].astype(jnp.float32) / (near_ref[...] + far_ref[...])
    rows, count = kernel_ref.shape
    group = 64

    def step(i, carry):
        at = pl.ds(pl.multiple_of(i * group, group), group)
        total = jnp.zeros((group, LANES), jnp.float32)
        for j in range(count // LANES):
            lanes = slice(j * LANES, (j + 1) * LANES)
            total = total + kernel_ref[at, lanes] * scale_ref[:, lanes]
        part[at, :] = total
        return carry

    lax.fori_loop(0, rows // group, step, 0)
    out_ref[...] = to_lanes(part[...])


def row_sums(kernel, near, far, counts):
    rows, count = kernel.shape
    return pl.pallas_call(
        row_body,
        out_shape=(
            jax.ShapeDtypeStruct((1, rows), jnp.float32),
            jax.ShapeDtypeStruct((1, count), jnp.float32),
        ),
        in_specs=whole(4),
        out_specs=tuple(whole(2)),
        scratch_shapes=[VMEM((rows, LANES), jnp.float32)],
        compiler_params=SMALL,
        name="row_sums",
    )(pltpu.with_memory_space_constraint(kernel, VMEM), near, far, counts)


def assign_body(kernel_ref, near_ref, far_ref, scale_ref, out_ref, spread, ready, sems):
    spread[...] = to_rows(1.0 / (near_ref[...] + far_ref[...]))
    stripes, group, count = ready.shape

    def put(i):
        return pltpu.make_async_copy(ready.at[i], out_ref.at[pl.ds(i * group, group), :], sems.at[i])

    def step(i, carry):
        at = pl.ds(pl.multiple_of(i * group, group), group)
        for j in range(count // LANES):
            lanes = slice(j * LANES, (j + 1) * LANES)
            value = spread[at, :] * kernel_ref[at, lanes] * scale_ref[:, lanes]
            ready[i, :, lanes] = value.astype(jnp.bfloat16)
        put(i).start()
        return carry

    lax.fori_loop(0, stripes, step, 0)
    for i in range(stripes):
        put(i).wait()


def assign(kernel, near, far, scale):
    rows, count = kernel.shape
    group = 64
    return pl.pallas_call(
        assign_body,
        out_shape=jax.ShapeDtypeStruct((rows, count), jnp.bfloat16),
        in_specs=whole(4),
        out_specs=pl.BlockSpec(memory_space=pl.ANY),
        scratch_shapes=[
            VMEM((rows, LANES), jnp.float32),
            VMEM((rows // group, group, count), jnp.bfloat16),
            pltpu.SemaphoreType.DMA((rows // group,)),
        ],
        compiler_params=SMALL,
        name="assign",
    )(pltpu.with_memory_space_constraint(kernel, VMEM), near, far, scale)


def shards(shapes, classes, counts):
    held, order = [shapes.T], [0]
    for bit in reversed(bits("cls")):
        held = held + [exchange(h, "cls", bit) for h in held]
        order = order + [o ^ bit for o in order]
    pieces = [held[order.index(o)] for o in range(len(held))]
    me = jnp.reshape(lax.axis_index("cls"), (1,)).astype(jnp.int32)
    class_f = classes.astype(jnp.float32)
    class_scale = lax.rsqrt(jnp.sum(class_f * class_f, axis=1) + epsilon)
    kernel, sums = make_kernel(me, pieces, class_scale[None, :], classes)
    target = counts[None, :]
    near, far = halves(sums, "cls")
    for step in range(ITERS):
        columns = halves(column_sums(kernel, near, far), "shape")
        sums, col_scale = row_sums(kernel, *columns, target)
        near, far = halves(sums, "cls")
    return assign(kernel, near, far, col_scale)


def solution(mesh):
    placed = (P("shape", "cls"), P("cls", None), P("cls"))
    return jax.shard_map(
        shards, mesh=mesh, in_specs=placed, out_specs=P("shape", "cls"), check_vma=False
    )
```

```python
import functools

import jax
import jax.numpy as jnp
from jax import lax
from jax.experimental import pallas as pl
from jax.experimental.pallas import tpu as pltpu
from jax.sharding import PartitionSpec as P

ITERS = 3

logit_scale = 40.0
epsilon = 1e-06
LANES = 128
VMEM = pltpu.VMEM
SMALL = pltpu.CompilerParams(vmem_limit_bytes=16 << 20)


def bits(axis):
    size = lax.axis_size(axis)
    assert size & (size - 1) == 0
    return [1 << b for b in range(size.bit_length() - 1)]


def exchange(value, axis, bit):
    size = lax.axis_size(axis)
    return lax.ppermute(value, axis, [(i, i ^ bit) for i in range(size)])


def halves(value, axis):
    steps = bits(axis)
    for bit in steps[:-1]:
        value = value + exchange(value, axis, bit)
    return value, exchange(value, axis, steps[-1])


def whole(count):
    return [pl.BlockSpec(memory_space=VMEM)] * count


def tile(index):
    return pl.ds(pl.multiple_of(index * LANES, LANES), LANES)


def to_lanes(value):
    return jnp.sum(value.T, axis=0, keepdims=True)


def to_rows(value):
    return jnp.broadcast_to(value, (LANES, value.shape[1])).T


def place(pieces, turned, me):
    depth = pieces[0].shape[0]
    for offset, piece in enumerate(pieces):
        slot = lax.bitwise_and(lax.bitwise_xor(me, offset), len(pieces) - 1)
        turned[pl.ds(pl.multiple_of(slot * depth, depth), depth), :] = piece[...]


def squares(value_ref, at=slice(None)):
    total = None
    for t in range(value_ref.shape[1] // LANES):
        value = value_ref[at, t * LANES : (t + 1) * LANES].astype(jnp.float32)
        total = value * value if total is None else total + value * value
    return total


def product(lhs, rhs):
    return lax.dot_general(lhs, rhs, (((1,), (1,)), ((), ())), preferred_element_type=jnp.float32)


def near_body(chunks, block, ahead, me_ref, *refs):
    pieces = refs[:chunks]
    classes_ref, products_ref, others_ref, scale_ref, square_ref, turned, lhs, held, sems = refs[chunks:]
    blocks = classes_ref.shape[0] // block
    width = lhs.shape[1]
    me = me_ref[0]
    mine = lax.div(me, chunks)

    def fetch(i):
        rows = pl.ds(pl.multiple_of(i * block, block), block)
        near = pl.ds(pl.multiple_of(mine * width, LANES), width)
        far = pl.ds(pl.multiple_of((1 - mine) * width, LANES), width)
        return (
            pltpu.make_async_copy(classes_ref.at[rows, near], held.at[rows, :], sems.at[0, i]),
            pltpu.make_async_copy(classes_ref.at[rows, far], others_ref.at[rows, :], sems.at[1, i]),
        )

    for i in range(min(ahead, blocks)):
        for copy in fetch(i):
            copy.start()
    place(pieces, turned, me)
    lhs[...] = turned[...].T
    square_ref[...] = squares(lhs)

    def step(i, carry):
        @pl.when(i + ahead < blocks)
        def _():
            for copy in fetch(i + ahead):
                copy.start()

        for copy in fetch(i):
            copy.wait()
        rows = pl.ds(pl.multiple_of(i * block, block), block)
        products_ref[:, rows] = product(lhs[...], held[rows, :])
        total = to_lanes(squares(held, rows) + squares(others_ref, rows))
        scale_ref[:, rows] = lax.rsqrt(total + epsilon)
        return carry

    lax.fori_loop(0, blocks, step, 0)


def block_of(count, tiles):
    total = count // LANES
    while total % tiles:
        tiles -= 1
    return tiles * LANES


def near_products(me, pieces, classes):
    count, features = classes.shape
    rows = pieces[0].shape[1]
    width = features // 2
    block = block_of(count, 8)
    return pl.pallas_call(
        functools.partial(near_body, len(pieces), block, 2),
        out_shape=(
            VMEM((rows, count), jnp.float32),
            VMEM((count, width), jnp.bfloat16),
            VMEM((1, count), jnp.float32),
            VMEM((rows, LANES), jnp.float32),
        ),
        in_specs=[pl.BlockSpec(memory_space=pltpu.SMEM)]
        + whole(len(pieces))
        + [pl.BlockSpec(memory_space=pl.ANY)],
        out_specs=tuple(whole(4)),
        scratch_shapes=[
            VMEM((width, rows), jnp.bfloat16),
            VMEM((rows, width), jnp.bfloat16),
            VMEM((count, width), jnp.bfloat16),
            pltpu.SemaphoreType.DMA((2, count // block)),
        ],
        cost_estimate=pl.CostEstimate(
            flops=2 * rows * count * width, bytes_accessed=2 * count * features, transcendentals=0
        ),
        compiler_params=pltpu.CompilerParams(vmem_limit_bytes=32 << 20),
        name="near_products",
    )(me, *pieces, classes)


def far_body(chunks, block, me_ref, *refs):
    pieces = refs[:chunks]
    products_ref, others_ref, scale_ref, square_ref, kernel_ref, sums_ref, turned, lhs, factor, part = refs[chunks:]
    place(pieces, turned, me_ref[0])
    lhs[...] = turned[...].T
    square = jnp.sum(square_ref[...] + squares(lhs), axis=1, keepdims=True)
    factor[...] = jnp.broadcast_to(logit_scale * lax.rsqrt(square + epsilon), factor.shape)
    part[...] = jnp.zeros_like(part)

    group = 64

    def step(i, carry):
        span = pl.ds(pl.multiple_of(i * block, block), block)
        view, scale = kernel_ref.at[:, span], scale_ref.at[:, span]
        view[...] = products_ref[:, span] + product(lhs[...], others_ref[span, :])
        for r in range(0, part.shape[0], group):
            rows = slice(r, r + group)
            total = part[rows, :]
            for at in range(0, block, LANES):
                lanes = slice(at, at + LANES)
                value = jnp.exp(view[rows, lanes] * factor[rows, :] * scale[:, lanes])
                view[rows, lanes] = value
                total = total + value
            part[rows, :] = total
        return carry

    lax.fori_loop(0, others_ref.shape[0] // block, step, 0)
    sums_ref[...] = to_lanes(part[...])


def far_kernel(me, pieces, products, others, scale, square):
    rows, count = products.shape
    width = others.shape[1]
    keep = pltpu.with_memory_space_constraint
    return pl.pallas_call(
        functools.partial(far_body, len(pieces), block_of(count, 20)),
        out_shape=(VMEM((rows, count), jnp.float32), VMEM((1, rows), jnp.float32)),
        in_specs=[pl.BlockSpec(memory_space=pltpu.SMEM)] + whole(len(pieces) + 4),
        out_specs=tuple(whole(2)),
        scratch_shapes=[
            VMEM((width, rows), jnp.bfloat16),
            VMEM((rows, width), jnp.bfloat16),
            VMEM((rows, LANES), jnp.float32),
            VMEM((rows, LANES), jnp.float32),
        ],
        input_output_aliases={1 + len(pieces): 0},
        compiler_params=pltpu.CompilerParams(vmem_limit_bytes=32 << 20),
        name="far_kernel",
    )(me, *pieces, keep(products, VMEM), keep(others, VMEM), keep(scale, VMEM), keep(square, VMEM))


def column_body(kernel_ref, near_ref, far_ref, out_ref, spread, part):
    spread[...] = to_rows(1.0 / (near_ref[...] + far_ref[...]))
    rows, count = kernel_ref.shape
    group = 64
    part[...] = jnp.zeros_like(part)

    def chunk(i, carry):
        at = pl.ds(pl.multiple_of(i * group, group), group)
        view, scale = kernel_ref.at[at, :], spread[at, :]
        for j in range(0, count, LANES):
            lanes = slice(j, j + LANES)
            value = (view[:, lanes] * scale).reshape(group // 8, 8, LANES)
            part[:, lanes] += jnp.sum(value, axis=0)
        return carry

    lax.fori_loop(0, rows // group, chunk, 0)
    out_ref[...] = jnp.sum(part[...], axis=0, keepdims=True)


def column_sums(kernel, near, far):
    rows, count = kernel.shape
    return pl.pallas_call(
        column_body,
        out_shape=jax.ShapeDtypeStruct((1, count), jnp.float32),
        in_specs=whole(3),
        out_specs=whole(1)[0],
        scratch_shapes=[VMEM((rows, LANES), jnp.float32), VMEM((8, count), jnp.float32)],
        compiler_params=SMALL,
        name="column_sums",
    )(pltpu.with_memory_space_constraint(kernel, VMEM), near, far)


def row_body(kernel_ref, near_ref, far_ref, counts_ref, out_ref, scale_ref, part):
    scale_ref[...] = counts_ref[...].astype(jnp.float32) / (near_ref[...] + far_ref[...])
    rows, count = kernel_ref.shape
    group, block = 64, block_of(count, 8)
    part[...] = jnp.zeros_like(part)

    def chunk(j, carry):
        span = pl.ds(pl.multiple_of(j * block, block), block)
        view, scale = kernel_ref.at[:, span], scale_ref.at[:, span]
        for r in range(0, rows, group):
            at = slice(r, r + group)
            total = part[at, :]
            for k in range(0, block, LANES):
                total = total + view[at, k : k + LANES] * scale[:, k : k + LANES]
            part[at, :] = total
        return carry

    lax.fori_loop(0, count // block, chunk, 0)
    out_ref[...] = to_lanes(part[...])


def row_sums(kernel, near, far, counts):
    rows, count = kernel.shape
    return pl.pallas_call(
        row_body,
        out_shape=(
            jax.ShapeDtypeStruct((1, rows), jnp.float32),
            jax.ShapeDtypeStruct((1, count), jnp.float32),
        ),
        in_specs=whole(4),
        out_specs=tuple(whole(2)),
        scratch_shapes=[VMEM((rows, LANES), jnp.float32)],
        compiler_params=SMALL,
        name="row_sums",
    )(pltpu.with_memory_space_constraint(kernel, VMEM), near, far, counts)


def assign_body(kernel_ref, near_ref, far_ref, scale_ref, out_ref, spread, ready, sems):
    spread[...] = to_rows(1.0 / (near_ref[...] + far_ref[...]))
    stripes, group, count = ready.shape

    def put(i):
        return pltpu.make_async_copy(ready.at[i], out_ref.at[pl.ds(i * group, group), :], sems.at[i])

    def step(i, carry):
        at = pl.ds(pl.multiple_of(i * group, group), group)
        for j in range(count // LANES):
            lanes = slice(j * LANES, (j + 1) * LANES)
            value = spread[at, :] * kernel_ref[at, lanes] * scale_ref[:, lanes]
            ready[i, :, lanes] = value.astype(jnp.bfloat16)
        put(i).start()
        return carry

    lax.fori_loop(0, stripes, step, 0)
    for i in range(stripes):
        put(i).wait()


def assign(kernel, near, far, scale):
    rows, count = kernel.shape
    group = 64
    return pl.pallas_call(
        assign_body,
        out_shape=jax.ShapeDtypeStruct((rows, count), jnp.bfloat16),
        in_specs=whole(4),
        out_specs=pl.BlockSpec(memory_space=pl.ANY),
        scratch_shapes=[
            VMEM((rows, LANES), jnp.float32),
            VMEM((rows // group, group, count), jnp.bfloat16),
            pltpu.SemaphoreType.DMA((rows // group,)),
        ],
        compiler_params=SMALL,
        name="assign",
    )(pltpu.with_memory_space_constraint(kernel, VMEM), near, far, scale)


def gathered(piece, steps):
    held = [piece]
    for bit in steps:
        held = held + [exchange(h, "cls", bit) for h in held]
    return held


def shards(shapes, classes, counts):
    *low, top = bits("cls")
    me = jnp.reshape(lax.axis_index("cls"), (1,)).astype(jnp.int32)
    mine = shapes.T
    other = exchange(mine, "cls", top)
    near = near_products(me, gathered(mine, low), classes)
    kernel, sums = far_kernel(me, gathered(other, low), *near)
    target = counts[None, :]
    near, far = halves(sums, "cls")
    for step in range(ITERS):
        columns = halves(column_sums(kernel, near, far), "shape")
        sums, col_scale = row_sums(kernel, *columns, target)
        near, far = halves(sums, "cls")
    return assign(kernel, near, far, col_scale)


def solution(mesh):
    placed = (P("shape", "cls"), P("cls", None), P("cls"))
    return jax.shard_map(
        shards, mesh=mesh, in_specs=placed, out_specs=P("shape", "cls"), check_vma=False
    )
```

```python
import functools

import jax
import jax.numpy as jnp
from jax import lax
from jax.experimental import pallas as pl
from jax.experimental.pallas import tpu as pltpu
from jax.sharding import PartitionSpec as P

ITERS = 3

logit_scale = 40.0
epsilon = 1e-06
LANES = 128
VMEM = pltpu.VMEM
SMALL = pltpu.CompilerParams(vmem_limit_bytes=16 << 20)


def bits(axis):
    size = lax.axis_size(axis)
    assert size & (size - 1) == 0
    return [1 << b for b in range(size.bit_length() - 1)]


def exchange(value, axis, bit):
    size = lax.axis_size(axis)
    return lax.ppermute(value, axis, [(i, i ^ bit) for i in range(size)])


def halves(value, axis):
    steps = bits(axis)
    for bit in steps[:-1]:
        value = value + exchange(value, axis, bit)
    return value, exchange(value, axis, steps[-1])


def whole(count):
    return [pl.BlockSpec(memory_space=VMEM)] * count


def tile(index):
    return pl.ds(pl.multiple_of(index * LANES, LANES), LANES)


def to_lanes(value):
    return jnp.sum(value.T, axis=0, keepdims=True)


def to_rows(value):
    return jnp.broadcast_to(value, (LANES, value.shape[1])).T


def place(pieces, turned, me):
    depth = pieces[0].shape[0]
    for offset, piece in enumerate(pieces):
        slot = lax.bitwise_and(lax.bitwise_xor(me, offset), len(pieces) - 1)
        turned[pl.ds(pl.multiple_of(slot * depth, depth), depth), :] = piece[...]


def squares(value_ref, at=slice(None)):
    total = None
    for t in range(value_ref.shape[1] // LANES):
        value = value_ref[at, t * LANES : (t + 1) * LANES].astype(jnp.float32)
        total = value * value if total is None else total + value * value
    return total


def product(lhs, rhs):
    return lax.dot_general(lhs, rhs, (((1,), (1,)), ((), ())), preferred_element_type=jnp.float32)


def near_body(block, ahead, first, last, mine, classes_ref, lhs, products_ref, others_ref, scale_ref, held, sems):
    width = lhs.shape[1]

    def fetch(i):
        rows = pl.ds(pl.multiple_of(i * block, block), block)
        near = pl.ds(pl.multiple_of(mine * width, LANES), width)
        far = pl.ds(pl.multiple_of((1 - mine) * width, LANES), width)
        return (
            pltpu.make_async_copy(classes_ref.at[rows, near], held.at[i - first], sems.at[0, i - first]),
            pltpu.make_async_copy(classes_ref.at[rows, far], others_ref.at[rows, :], sems.at[1, i - first]),
        )

    def begin():
        for i in range(first, min(first + ahead, last)):
            for copy in fetch(i):
                copy.start()

    def step(i, carry):
        @pl.when(i + ahead < last)
        def _():
            for copy in fetch(i + ahead):
                copy.start()

        for copy in fetch(i):
            copy.wait()
        rows = pl.ds(pl.multiple_of(i * block, block), block)
        products_ref[:, rows] = product(lhs[...], held[i - first])
        total = to_lanes(squares(held.at[i - first]) + squares(others_ref, rows))
        scale_ref[:, rows] = lax.rsqrt(total + epsilon)
        return carry

    return begin, lambda: lax.fori_loop(first, last, step, 0)


def first_body(chunks, block, ahead, last, me_ref, *refs):
    pieces = refs[:chunks]
    classes_ref, products_ref, others_ref, scale_ref, square_ref, lhs, turned, held, sems = refs[chunks:]
    me = me_ref[0]
    begin, run = near_body(
        block, ahead, 0, last, lax.div(me, chunks), classes_ref, lhs, products_ref, others_ref, scale_ref, held, sems
    )
    begin()
    place(pieces, turned, me)
    lhs[...] = turned[...].T
    square_ref[...] = squares(lhs)
    run()


def second_body(chunks, block, ahead, first, last, me_ref, lhs, classes_ref, *refs):
    products_ref, others_ref, scale_ref, held, sems = refs[3:]
    begin, run = near_body(
        block, ahead, first, last, lax.div(me_ref[0], chunks), classes_ref, lhs, products_ref, others_ref, scale_ref, held, sems
    )
    begin()
    run()


def block_of(count, tiles):
    total = count // LANES
    while total % tiles:
        tiles -= 1
    return tiles * LANES


def near_products(me, pieces, classes):
    count, features = classes.shape
    chunks, rows = len(pieces), pieces[0].shape[1]
    width = features // 2
    block = block_of(count, 8)
    blocks = count // block
    split = blocks - blocks // 4 if blocks > 1 else blocks

    def cost(part):
        return pl.CostEstimate(
            flops=2 * rows * part * block * width, bytes_accessed=2 * part * block * features, transcendentals=0
        )

    def scratch(part):
        return [VMEM((part, block, width), jnp.bfloat16), pltpu.SemaphoreType.DMA((2, part))]

    keep = pltpu.with_memory_space_constraint
    scalar, plain = [pl.BlockSpec(memory_space=pltpu.SMEM)], [pl.BlockSpec(memory_space=pl.ANY)]
    shared = (
        VMEM((rows, count), jnp.float32),
        VMEM((count, width), jnp.bfloat16),
        VMEM((1, count), jnp.float32),
    )
    *parts, square, lhs = pl.pallas_call(
        functools.partial(first_body, chunks, block, 2, split),
        out_shape=shared + (VMEM((rows, LANES), jnp.float32), VMEM((rows, width), jnp.bfloat16)),
        in_specs=scalar + whole(chunks) + plain,
        out_specs=tuple(whole(5)),
        scratch_shapes=[VMEM((width, rows), jnp.bfloat16)] + scratch(split),
        cost_estimate=cost(split),
        compiler_params=pltpu.CompilerParams(vmem_limit_bytes=32 << 20),
        name="near_first",
    )(me, *pieces, classes)

    def rest(lhs):
        if split == blocks:
            return (*parts, square)
        done = pl.pallas_call(
            functools.partial(second_body, chunks, block, 2, split, blocks),
            out_shape=shared,
            in_specs=scalar + whole(1) + plain + whole(3),
            out_specs=tuple(whole(3)),
            scratch_shapes=scratch(blocks - split),
            input_output_aliases={3: 0, 4: 1, 5: 2},
            cost_estimate=cost(blocks - split),
            compiler_params=pltpu.CompilerParams(vmem_limit_bytes=24 << 20),
            name="near_second",
        )(me, keep(lhs, VMEM), classes, *(keep(p, VMEM) for p in parts))
        return (*done, square)

    return lhs, rest


def far_body(chunks, block, me_ref, *refs):
    pieces = refs[:chunks]
    products_ref, others_ref, scale_ref, square_ref, kernel_ref, sums_ref, turned, lhs, factor, part = refs[chunks:]
    place(pieces, turned, me_ref[0])
    lhs[...] = turned[...].T
    square = jnp.sum(square_ref[...] + squares(lhs), axis=1, keepdims=True)
    factor[...] = jnp.broadcast_to(logit_scale * lax.rsqrt(square + epsilon), factor.shape)
    part[...] = jnp.zeros_like(part)

    group = 64

    def step(i, carry):
        span = pl.ds(pl.multiple_of(i * block, block), block)
        view, scale = kernel_ref.at[:, span], scale_ref.at[:, span]
        view[...] = products_ref[:, span] + product(lhs[...], others_ref[span, :])
        for r in range(0, part.shape[0], group):
            rows = slice(r, r + group)
            total = part[rows, :]
            for at in range(0, block, LANES):
                lanes = slice(at, at + LANES)
                value = jnp.exp(view[rows, lanes] * factor[rows, :] * scale[:, lanes])
                view[rows, lanes] = value
                total = total + value
            part[rows, :] = total
        return carry

    lax.fori_loop(0, others_ref.shape[0] // block, step, 0)
    sums_ref[...] = to_lanes(part[...])


def far_kernel(me, pieces, products, others, scale, square):
    rows, count = products.shape
    width = others.shape[1]
    keep = pltpu.with_memory_space_constraint
    return pl.pallas_call(
        functools.partial(far_body, len(pieces), block_of(count, 20)),
        out_shape=(VMEM((rows, count), jnp.float32), VMEM((1, rows), jnp.float32)),
        in_specs=[pl.BlockSpec(memory_space=pltpu.SMEM)] + whole(len(pieces) + 4),
        out_specs=tuple(whole(2)),
        scratch_shapes=[
            VMEM((width, rows), jnp.bfloat16),
            VMEM((rows, width), jnp.bfloat16),
            VMEM((rows, LANES), jnp.float32),
            VMEM((rows, LANES), jnp.float32),
        ],
        input_output_aliases={1 + len(pieces): 0},
        compiler_params=pltpu.CompilerParams(vmem_limit_bytes=32 << 20),
        name="far_kernel",
    )(me, *pieces, keep(products, VMEM), keep(others, VMEM), keep(scale, VMEM), keep(square, VMEM))


def column_body(kernel_ref, near_ref, far_ref, out_ref, spread, part):
    spread[...] = to_rows(1.0 / (near_ref[...] + far_ref[...]))
    rows, count = kernel_ref.shape
    group = 64
    part[...] = jnp.zeros_like(part)

    def chunk(i, carry):
        at = pl.ds(pl.multiple_of(i * group, group), group)
        view, scale = kernel_ref.at[at, :], spread[at, :]
        for j in range(0, count, LANES):
            lanes = slice(j, j + LANES)
            value = (view[:, lanes] * scale).reshape(group // 8, 8, LANES)
            part[:, lanes] += jnp.sum(value, axis=0)
        return carry

    lax.fori_loop(0, rows // group, chunk, 0)
    out_ref[...] = jnp.sum(part[...], axis=0, keepdims=True)


def column_sums(kernel, near, far):
    rows, count = kernel.shape
    return pl.pallas_call(
        column_body,
        out_shape=jax.ShapeDtypeStruct((1, count), jnp.float32),
        in_specs=whole(3),
        out_specs=whole(1)[0],
        scratch_shapes=[VMEM((rows, LANES), jnp.float32), VMEM((8, count), jnp.float32)],
        compiler_params=SMALL,
        name="column_sums",
    )(pltpu.with_memory_space_constraint(kernel, VMEM), near, far)


def row_body(kernel_ref, near_ref, far_ref, counts_ref, out_ref, scale_ref, part):
    scale_ref[...] = counts_ref[...].astype(jnp.float32) / (near_ref[...] + far_ref[...])
    rows, count = kernel_ref.shape
    group, block = 64, block_of(count, 8)
    part[...] = jnp.zeros_like(part)

    def chunk(j, carry):
        span = pl.ds(pl.multiple_of(j * block, block), block)
        view, scale = kernel_ref.at[:, span], scale_ref.at[:, span]
        for r in range(0, rows, group):
            at = slice(r, r + group)
            total = part[at, :]
            for k in range(0, block, LANES):
                total = total + view[at, k : k + LANES] * scale[:, k : k + LANES]
            part[at, :] = total
        return carry

    lax.fori_loop(0, count // block, chunk, 0)
    out_ref[...] = to_lanes(part[...])


def row_sums(kernel, near, far, counts):
    rows, count = kernel.shape
    return pl.pallas_call(
        row_body,
        out_shape=(
            jax.ShapeDtypeStruct((1, rows), jnp.float32),
            jax.ShapeDtypeStruct((1, count), jnp.float32),
        ),
        in_specs=whole(4),
        out_specs=tuple(whole(2)),
        scratch_shapes=[VMEM((rows, LANES), jnp.float32)],
        compiler_params=SMALL,
        name="row_sums",
    )(pltpu.with_memory_space_constraint(kernel, VMEM), near, far, counts)


def assign_body(kernel_ref, near_ref, far_ref, scale_ref, out_ref, spread, ready, sems):
    spread[...] = to_rows(1.0 / (near_ref[...] + far_ref[...]))
    stripes, group, count = ready.shape

    def put(i):
        return pltpu.make_async_copy(ready.at[i], out_ref.at[pl.ds(i * group, group), :], sems.at[i])

    def step(i, carry):
        at = pl.ds(pl.multiple_of(i * group, group), group)
        for j in range(count // LANES):
            lanes = slice(j * LANES, (j + 1) * LANES)
            value = spread[at, :] * kernel_ref[at, lanes] * scale_ref[:, lanes]
            ready[i, :, lanes] = value.astype(jnp.bfloat16)
        put(i).start()
        return carry

    lax.fori_loop(0, stripes, step, 0)
    for i in range(stripes):
        put(i).wait()


def assign(kernel, near, far, scale):
    rows, count = kernel.shape
    group = 64
    return pl.pallas_call(
        assign_body,
        out_shape=jax.ShapeDtypeStruct((rows, count), jnp.bfloat16),
        in_specs=whole(4),
        out_specs=pl.BlockSpec(memory_space=pl.ANY),
        scratch_shapes=[
            VMEM((rows, LANES), jnp.float32),
            VMEM((rows // group, group, count), jnp.bfloat16),
            pltpu.SemaphoreType.DMA((rows // group,)),
        ],
        compiler_params=SMALL,
        name="assign",
    )(pltpu.with_memory_space_constraint(kernel, VMEM), near, far, scale)


def gathered(piece, steps):
    held = [piece]
    for bit in steps:
        held = held + [exchange(h, "cls", bit) for h in held]
    return held


def shards(shapes, classes, counts):
    *low, top = bits("cls")
    me = jnp.reshape(lax.axis_index("cls"), (1,)).astype(jnp.int32)
    mine = shapes.T
    other = exchange(mine, "cls", top)
    lhs, rest = near_products(me, gathered(mine, low), classes)
    lhs, other = lax.optimization_barrier((lhs, other))
    pieces = gathered(other, low)
    kernel, sums = far_kernel(me, pieces, *rest(lhs))
    target = counts[None, :]
    near, far = halves(sums, "cls")
    for step in range(ITERS):
        columns = halves(column_sums(kernel, near, far), "shape")
        sums, col_scale = row_sums(kernel, *columns, target)
        near, far = halves(sums, "cls")
    return assign(kernel, near, far, col_scale)


def solution(mesh):
    placed = (P("shape", "cls"), P("cls", None), P("cls"))
    return jax.shard_map(
        shards, mesh=mesh, in_specs=placed, out_specs=P("shape", "cls"), check_vma=False
    )
```

```python
import functools

import jax
import jax.numpy as jnp
from jax import lax
from jax.experimental import pallas as pl
from jax.experimental.pallas import tpu as pltpu
from jax.sharding import PartitionSpec as P

ITERS = 3

logit_scale = 40.0
epsilon = 1e-06
LANES = 128
VMEM = pltpu.VMEM
SMALL = pltpu.CompilerParams(vmem_limit_bytes=16 << 20)


def bits(axis):
    size = lax.axis_size(axis)
    assert size & (size - 1) == 0
    return [1 << b for b in range(size.bit_length() - 1)]


def exchange(value, axis, bit):
    size = lax.axis_size(axis)
    return lax.ppermute(value, axis, [(i, i ^ bit) for i in range(size)])


def halves(value, axis):
    steps = bits(axis)
    for bit in steps[:-1]:
        value = value + exchange(value, axis, bit)
    return value, exchange(value, axis, steps[-1])


def whole(count):
    return [pl.BlockSpec(memory_space=VMEM)] * count


def tile(index):
    return pl.ds(pl.multiple_of(index * LANES, LANES), LANES)


def to_lanes(value):
    return jnp.sum(value.T, axis=0, keepdims=True)


def to_rows(value):
    return jnp.broadcast_to(value, (LANES, value.shape[1])).T


def slot(pieces, turned, me, offset):
    depth = turned.shape[0] // pieces
    index = lax.bitwise_and(lax.bitwise_xor(me, offset), pieces - 1)
    return turned.at[pl.ds(pl.multiple_of(index * depth, depth), depth), :]


def place(pieces, turned, me, start=0):
    for offset in range(start, len(pieces)):
        slot(len(pieces), turned, me, offset)[...] = pieces[offset][...]


def squares(value_ref, at=slice(None)):
    total = None
    for t in range(value_ref.shape[1] // LANES):
        value = value_ref[at, t * LANES : (t + 1) * LANES].astype(jnp.float32)
        total = value * value if total is None else total + value * value
    return total


def product(lhs, rhs):
    return lax.dot_general(lhs, rhs, (((1,), (1,)), ((), ())), preferred_element_type=jnp.float32)


def near_body(block, ahead, first, last, mine, classes_ref, lhs, products_ref, others_ref, scale_ref, held, sems):
    width = lhs.shape[1]

    def fetch(i):
        rows = pl.ds(pl.multiple_of(i * block, block), block)
        near = pl.ds(pl.multiple_of(mine * width, LANES), width)
        far = pl.ds(pl.multiple_of((1 - mine) * width, LANES), width)
        return (
            pltpu.make_async_copy(classes_ref.at[rows, near], held.at[i - first], sems.at[0, i - first]),
            pltpu.make_async_copy(classes_ref.at[rows, far], others_ref.at[rows, :], sems.at[1, i - first]),
        )

    def begin():
        for i in range(first, min(first + ahead, last)):
            for copy in fetch(i):
                copy.start()

    def step(i, carry):
        @pl.when(i + ahead < last)
        def _():
            for copy in fetch(i + ahead):
                copy.start()

        for copy in fetch(i):
            copy.wait()
        rows = pl.ds(pl.multiple_of(i * block, block), block)
        products_ref[:, rows] = product(lhs[...], held[i - first])
        total = to_lanes(squares(held.at[i - first]) + squares(others_ref, rows))
        scale_ref[:, rows] = lax.rsqrt(total + epsilon)
        return carry

    return begin, lambda: lax.fori_loop(first, last, step, 0)


def first_body(chunks, block, ahead, last, me_ref, *refs):
    pieces = refs[:chunks]
    classes_ref, products_ref, others_ref, scale_ref, square_ref, lhs, turned, own, held, sems = refs[chunks:]
    me = me_ref[0]
    copy = pltpu.make_async_copy(pieces[0], slot(chunks, turned, me, 0), own)
    copy.start()
    begin, run = near_body(
        block, ahead, 0, last, lax.div(me, chunks), classes_ref, lhs, products_ref, others_ref, scale_ref, held, sems
    )
    begin()
    place(pieces, turned, me, 1)
    copy.wait()
    lhs[...] = turned[...].T
    square_ref[...] = squares(lhs)
    run()


def second_body(chunks, block, ahead, first, last, me_ref, lhs, classes_ref, *refs):
    products_ref, others_ref, scale_ref, held, sems = refs[3:]
    begin, run = near_body(
        block, ahead, first, last, lax.div(me_ref[0], chunks), classes_ref, lhs, products_ref, others_ref, scale_ref, held, sems
    )
    begin()
    run()


def block_of(count, tiles):
    total = count // LANES
    while total % tiles:
        tiles -= 1
    return tiles * LANES


def near_products(me, pieces, classes):
    count, features = classes.shape
    chunks, rows = len(pieces), pieces[0].shape[1]
    width = features // 2
    block = block_of(count, 8)
    blocks = count // block
    split = blocks - blocks // 4 if blocks > 1 else blocks

    def cost(part):
        return pl.CostEstimate(
            flops=2 * rows * part * block * width, bytes_accessed=2 * part * block * features, transcendentals=0
        )

    def scratch(part):
        return [VMEM((part, block, width), jnp.bfloat16), pltpu.SemaphoreType.DMA((2, part))]

    keep = pltpu.with_memory_space_constraint
    scalar, plain = [pl.BlockSpec(memory_space=pltpu.SMEM)], [pl.BlockSpec(memory_space=pltpu.HBM)]
    classes = keep(classes, pltpu.HBM)
    shared = (
        VMEM((rows, count), jnp.float32),
        VMEM((count, width), jnp.bfloat16),
        VMEM((1, count), jnp.float32),
    )
    *parts, square, lhs = pl.pallas_call(
        functools.partial(first_body, chunks, block, 2, split),
        out_shape=shared + (VMEM((rows, LANES), jnp.float32), VMEM((rows, width), jnp.bfloat16)),
        in_specs=scalar + plain + whole(chunks - 1) + plain,
        out_specs=tuple(whole(5)),
        scratch_shapes=[VMEM((width, rows), jnp.bfloat16), pltpu.SemaphoreType.DMA(())] + scratch(split),
        cost_estimate=cost(split),
        compiler_params=pltpu.CompilerParams(vmem_limit_bytes=32 << 20),
        name="near_first",
    )(me, keep(pieces[0], pltpu.HBM), *(keep(p, VMEM) for p in pieces[1:]), classes)

    def rest(lhs):
        if split == blocks:
            return (*parts, square)
        done = pl.pallas_call(
            functools.partial(second_body, chunks, block, 2, split, blocks),
            out_shape=shared,
            in_specs=scalar + whole(1) + plain + whole(3),
            out_specs=tuple(whole(3)),
            scratch_shapes=scratch(blocks - split),
            input_output_aliases={3: 0, 4: 1, 5: 2},
            cost_estimate=cost(blocks - split),
            compiler_params=pltpu.CompilerParams(vmem_limit_bytes=24 << 20),
            name="near_second",
        )(me, keep(lhs, VMEM), classes, *(keep(p, VMEM) for p in parts))
        return (*done, square)

    return lhs, rest


def far_body(chunks, block, me_ref, *refs):
    pieces = refs[:chunks]
    products_ref, others_ref, scale_ref, square_ref, kernel_ref, sums_ref, turned, lhs, factor, part = refs[chunks:]
    place(pieces, turned, me_ref[0])
    lhs[...] = turned[...].T
    square = jnp.sum(square_ref[...] + squares(lhs), axis=1, keepdims=True)
    factor[...] = jnp.broadcast_to(logit_scale * lax.rsqrt(square + epsilon), factor.shape)
    part[...] = jnp.zeros_like(part)

    group = 64

    def step(i, carry):
        span = pl.ds(pl.multiple_of(i * block, block), block)
        view, scale = kernel_ref.at[:, span], scale_ref.at[:, span]
        view[...] = products_ref[:, span] + product(lhs[...], others_ref[span, :])
        for r in range(0, part.shape[0], group):
            rows = slice(r, r + group)
            total = part[rows, :]
            for at in range(0, block, LANES):
                lanes = slice(at, at + LANES)
                value = jnp.exp(view[rows, lanes] * factor[rows, :] * scale[:, lanes])
                view[rows, lanes] = value
                total = total + value
            part[rows, :] = total
        return carry

    lax.fori_loop(0, others_ref.shape[0] // block, step, 0)
    sums_ref[...] = to_lanes(part[...])


def far_kernel(me, pieces, products, others, scale, square):
    rows, count = products.shape
    width = others.shape[1]
    keep = pltpu.with_memory_space_constraint
    return pl.pallas_call(
        functools.partial(far_body, len(pieces), block_of(count, 20)),
        out_shape=(VMEM((rows, count), jnp.float32), VMEM((1, rows), jnp.float32)),
        in_specs=[pl.BlockSpec(memory_space=pltpu.SMEM)] + whole(len(pieces) + 4),
        out_specs=tuple(whole(2)),
        scratch_shapes=[
            VMEM((width, rows), jnp.bfloat16),
            VMEM((rows, width), jnp.bfloat16),
            VMEM((rows, LANES), jnp.float32),
            VMEM((rows, LANES), jnp.float32),
        ],
        input_output_aliases={1 + len(pieces): 0},
        compiler_params=pltpu.CompilerParams(vmem_limit_bytes=32 << 20),
        name="far_kernel",
    )(me, *(keep(p, VMEM) for p in pieces), keep(products, VMEM), keep(others, VMEM), keep(scale, VMEM), keep(square, VMEM))


def column_body(kernel_ref, near_ref, far_ref, out_ref, spread, part):
    spread[...] = to_rows(1.0 / (near_ref[...] + far_ref[...]))
    rows, count = kernel_ref.shape
    group = 64
    part[...] = jnp.zeros_like(part)

    def chunk(i, carry):
        at = pl.ds(pl.multiple_of(i * group, group), group)
        view, scale = kernel_ref.at[at, :], spread[at, :]
        for j in range(0, count, LANES):
            lanes = slice(j, j + LANES)
            value = (view[:, lanes] * scale).reshape(group // 8, 8, LANES)
            part[:, lanes] += jnp.sum(value, axis=0)
        return carry

    lax.fori_loop(0, rows // group, chunk, 0)
    out_ref[...] = jnp.sum(part[...], axis=0, keepdims=True)


def column_sums(kernel, near, far):
    rows, count = kernel.shape
    return pl.pallas_call(
        column_body,
        out_shape=jax.ShapeDtypeStruct((1, count), jnp.float32),
        in_specs=whole(3),
        out_specs=whole(1)[0],
        scratch_shapes=[VMEM((rows, LANES), jnp.float32), VMEM((8, count), jnp.float32)],
        compiler_params=SMALL,
        name="column_sums",
    )(pltpu.with_memory_space_constraint(kernel, VMEM), near, far)


def row_body(kernel_ref, near_ref, far_ref, counts_ref, out_ref, scale_ref, part):
    scale_ref[...] = counts_ref[...].astype(jnp.float32) / (near_ref[...] + far_ref[...])
    rows, count = kernel_ref.shape
    group, block = 64, block_of(count, 8)
    part[...] = jnp.zeros_like(part)

    def chunk(j, carry):
        span = pl.ds(pl.multiple_of(j * block, block), block)
        view, scale = kernel_ref.at[:, span], scale_ref.at[:, span]
        for r in range(0, rows, group):
            at = slice(r, r + group)
            total = part[at, :]
            for k in range(0, block, LANES):
                total = total + view[at, k : k + LANES] * scale[:, k : k + LANES]
            part[at, :] = total
        return carry

    lax.fori_loop(0, count // block, chunk, 0)
    out_ref[...] = to_lanes(part[...])


def row_sums(kernel, near, far, counts):
    rows, count = kernel.shape
    return pl.pallas_call(
        row_body,
        out_shape=(
            jax.ShapeDtypeStruct((1, rows), jnp.float32),
            jax.ShapeDtypeStruct((1, count), jnp.float32),
        ),
        in_specs=whole(4),
        out_specs=tuple(whole(2)),
        scratch_shapes=[VMEM((rows, LANES), jnp.float32)],
        compiler_params=SMALL,
        name="row_sums",
    )(pltpu.with_memory_space_constraint(kernel, VMEM), near, far, counts)


def assign_body(kernel_ref, near_ref, far_ref, scale_ref, out_ref, spread, ready, sems):
    spread[...] = to_rows(1.0 / (near_ref[...] + far_ref[...]))
    stripes, group, count = ready.shape

    def put(i):
        return pltpu.make_async_copy(ready.at[i], out_ref.at[pl.ds(i * group, group), :], sems.at[i])

    def step(i, carry):
        at = pl.ds(pl.multiple_of(i * group, group), group)
        for j in range(count // LANES):
            lanes = slice(j * LANES, (j + 1) * LANES)
            value = spread[at, :] * kernel_ref[at, lanes] * scale_ref[:, lanes]
            ready[i, :, lanes] = value.astype(jnp.bfloat16)
        put(i).start()
        return carry

    lax.fori_loop(0, stripes, step, 0)
    for i in range(stripes):
        put(i).wait()


def assign(kernel, near, far, scale):
    rows, count = kernel.shape
    group = 64
    return pl.pallas_call(
        assign_body,
        out_shape=jax.ShapeDtypeStruct((rows, count), jnp.bfloat16),
        in_specs=whole(4),
        out_specs=pl.BlockSpec(memory_space=pl.ANY),
        scratch_shapes=[
            VMEM((rows, LANES), jnp.float32),
            VMEM((rows // group, group, count), jnp.bfloat16),
            pltpu.SemaphoreType.DMA((rows // group,)),
        ],
        compiler_params=SMALL,
        name="assign",
    )(pltpu.with_memory_space_constraint(kernel, VMEM), near, far, scale)


def gathered(piece, steps):
    held = [piece]
    for bit in steps:
        held = held + [exchange(h, "cls", bit) for h in held]
    return held


def shards(shapes, classes, counts):
    *low, top = bits("cls")
    me = jnp.reshape(lax.axis_index("cls"), (1,)).astype(jnp.int32)
    mine = shapes.T
    other = exchange(mine, "cls", top)
    lhs, rest = near_products(me, gathered(mine, low), classes)
    lhs, other = lax.optimization_barrier((lhs, other))
    pieces = gathered(other, low)
    kernel, sums = far_kernel(me, pieces, *rest(lhs))
    target = counts[None, :]
    near, far = halves(sums, "cls")
    for step in range(ITERS):
        columns = halves(column_sums(kernel, near, far), "shape")
        sums, col_scale = row_sums(kernel, *columns, target)
        near, far = halves(sums, "cls")
    return assign(kernel, near, far, col_scale)


def solution(mesh):
    placed = (P("shape", "cls"), P("cls", None), P("cls"))
    return jax.shard_map(
        shards, mesh=mesh, in_specs=placed, out_specs=P("shape", "cls"), check_vma=False
    )
```

```python
import functools

import jax
import jax.numpy as jnp
from jax import lax
from jax.experimental import pallas as pl
from jax.experimental.pallas import tpu as pltpu
from jax.sharding import PartitionSpec as P

ITERS = 3

logit_scale = 40.0
epsilon = 1e-06
LANES = 128
VMEM = pltpu.VMEM
SMALL = pltpu.CompilerParams(vmem_limit_bytes=16 << 20)


def bits(axis):
    size = lax.axis_size(axis)
    assert size & (size - 1) == 0
    return [1 << b for b in range(size.bit_length() - 1)]


def exchange(value, axis, bit):
    size = lax.axis_size(axis)
    return lax.ppermute(value, axis, [(i, i ^ bit) for i in range(size)])


def terms(value, axis):
    parts, steps = [value], bits(axis)
    for at in range(0, len(steps), 2):
        value = sum(parts[1:], parts[0])
        offsets = [0]
        for bit in steps[at : at + 2]:
            offsets = offsets + [o ^ bit for o in offsets]
        parts = [value] + [exchange(value, axis, o) for o in offsets[1:]]
    return parts


def spread_out(value, axis):
    copies = jnp.broadcast_to(value[None], (lax.axis_size(axis),) + value.shape)
    return lax.all_to_all(copies, axis, 0, 0)


def whole(count):
    return [pl.BlockSpec(memory_space=VMEM)] * count


def tile(index):
    return pl.ds(pl.multiple_of(index * LANES, LANES), LANES)


def to_lanes(value):
    return jnp.sum(value.T, axis=0, keepdims=True)


def to_rows(value):
    return jnp.broadcast_to(value, (LANES, value.shape[1])).T


def slot(pieces, turned, me, offset):
    depth = turned.shape[0] // pieces
    index = lax.bitwise_and(lax.bitwise_xor(me, offset), pieces - 1)
    return turned.at[pl.ds(pl.multiple_of(index * depth, depth), depth), :]


def place(pieces, turned, me, start=0):
    for offset in range(start, len(pieces)):
        slot(len(pieces), turned, me, offset)[...] = pieces[offset][...]


def squares(value_ref, at=slice(None)):
    total = None
    for t in range(value_ref.shape[1] // LANES):
        value = value_ref[at, t * LANES : (t + 1) * LANES].astype(jnp.float32)
        total = value * value if total is None else total + value * value
    return total


def product(lhs, rhs):
    return lax.dot_general(lhs, rhs, (((1,), (1,)), ((), ())), preferred_element_type=jnp.float32)


def near_body(block, ahead, first, last, mine, classes_ref, lhs, products_ref, others_ref, scale_ref, held, sems):
    width = lhs.shape[1]

    def fetch(i):
        rows = pl.ds(pl.multiple_of(i * block, block), block)
        near = pl.ds(pl.multiple_of(mine * width, LANES), width)
        far = pl.ds(pl.multiple_of((1 - mine) * width, LANES), width)
        return (
            pltpu.make_async_copy(classes_ref.at[rows, near], held.at[i - first], sems.at[0, i - first]),
            pltpu.make_async_copy(classes_ref.at[rows, far], others_ref.at[rows, :], sems.at[1, i - first]),
        )

    def begin():
        for i in range(first, min(first + ahead, last)):
            for copy in fetch(i):
                copy.start()

    def step(i, carry):
        @pl.when(i + ahead < last)
        def _():
            for copy in fetch(i + ahead):
                copy.start()

        for copy in fetch(i):
            copy.wait()
        rows = pl.ds(pl.multiple_of(i * block, block), block)
        products_ref[:, rows] = product(lhs[...], held[i - first])
        total = to_lanes(squares(held.at[i - first]) + squares(others_ref, rows))
        scale_ref[:, rows] = lax.rsqrt(total + epsilon)
        return carry

    return begin, lambda: lax.fori_loop(first, last, step, 0)


def first_body(chunks, block, ahead, last, me_ref, *refs):
    pieces = refs[:chunks]
    classes_ref, products_ref, others_ref, scale_ref, square_ref, lhs, turned, own, held, sems = refs[chunks:]
    me = me_ref[0]
    copy = pltpu.make_async_copy(pieces[0], slot(chunks, turned, me, 0), own)
    copy.start()
    begin, run = near_body(
        block, ahead, 0, last, lax.div(me, chunks), classes_ref, lhs, products_ref, others_ref, scale_ref, held, sems
    )
    begin()
    place(pieces, turned, me, 1)
    copy.wait()
    lhs[...] = turned[...].T
    square_ref[...] = squares(lhs)
    run()


def second_body(chunks, block, ahead, first, last, me_ref, lhs, classes_ref, *refs):
    products_ref, others_ref, scale_ref, held, sems = refs[3:]
    begin, run = near_body(
        block, ahead, first, last, lax.div(me_ref[0], chunks), classes_ref, lhs, products_ref, others_ref, scale_ref, held, sems
    )
    begin()
    run()


def block_of(count, tiles):
    total = count // LANES
    while total % tiles:
        tiles -= 1
    return tiles * LANES


def near_products(me, pieces, classes):
    count, features = classes.shape
    chunks, rows = len(pieces), pieces[0].shape[1]
    width = features // 2
    block = block_of(count, 8)
    blocks = count // block
    split = blocks

    def cost(part):
        return pl.CostEstimate(
            flops=2 * rows * part * block * width, bytes_accessed=2 * part * block * features, transcendentals=0
        )

    def scratch(part):
        return [VMEM((part, block, width), jnp.bfloat16), pltpu.SemaphoreType.DMA((2, part))]

    keep = pltpu.with_memory_space_constraint
    scalar, plain = [pl.BlockSpec(memory_space=pltpu.SMEM)], [pl.BlockSpec(memory_space=pltpu.HBM)]
    classes = keep(classes, pltpu.HBM)
    shared = (
        VMEM((rows, count), jnp.float32),
        VMEM((count, width), jnp.bfloat16),
        VMEM((1, count), jnp.float32),
    )
    *parts, square, lhs = pl.pallas_call(
        functools.partial(first_body, chunks, block, 2, split),
        out_shape=shared + (VMEM((rows, LANES), jnp.float32), VMEM((rows, width), jnp.bfloat16)),
        in_specs=scalar + plain + whole(chunks - 1) + plain,
        out_specs=tuple(whole(5)),
        scratch_shapes=[VMEM((width, rows), jnp.bfloat16), pltpu.SemaphoreType.DMA(())] + scratch(split),
        cost_estimate=cost(split),
        compiler_params=pltpu.CompilerParams(vmem_limit_bytes=32 << 20),
        name="near_first",
    )(me, keep(pieces[0], pltpu.HBM), *(keep(p, VMEM) for p in pieces[1:]), classes)

    def rest(lhs):
        if split == blocks:
            return (*parts, square)
        done = pl.pallas_call(
            functools.partial(second_body, chunks, block, 2, split, blocks),
            out_shape=shared,
            in_specs=scalar + whole(1) + plain + whole(3),
            out_specs=tuple(whole(3)),
            scratch_shapes=scratch(blocks - split),
            input_output_aliases={3: 0, 4: 1, 5: 2},
            cost_estimate=cost(blocks - split),
            compiler_params=pltpu.CompilerParams(vmem_limit_bytes=24 << 20),
            name="near_second",
        )(me, keep(lhs, VMEM), classes, *(keep(p, VMEM) for p in parts))
        return (*done, square)

    return lhs, rest


def far_body(chunks, block, me_ref, *refs):
    pieces = refs[:chunks]
    products_ref, others_ref, scale_ref, square_ref, kernel_ref, sums_ref, turned, lhs, factor, part = refs[chunks:]
    place(pieces, turned, me_ref[0])
    lhs[...] = turned[...].T
    square = jnp.sum(square_ref[...] + squares(lhs), axis=1, keepdims=True)
    factor[...] = jnp.broadcast_to(logit_scale * lax.rsqrt(square + epsilon), factor.shape)
    part[...] = jnp.zeros_like(part)

    group = 64

    def step(i, carry):
        span = pl.ds(pl.multiple_of(i * block, block), block)
        view, scale = kernel_ref.at[:, span], scale_ref.at[:, span]
        view[...] = products_ref[:, span] + product(lhs[...], others_ref[span, :])
        for r in range(0, part.shape[0], group):
            rows = slice(r, r + group)
            total = part[rows, :]
            for at in range(0, block, LANES):
                lanes = slice(at, at + LANES)
                value = jnp.exp(view[rows, lanes] * factor[rows, :] * scale[:, lanes])
                view[rows, lanes] = value
                total = total + value
            part[rows, :] = total
        return carry

    lax.fori_loop(0, others_ref.shape[0] // block, step, 0)
    sums_ref[...] = to_lanes(part[...])


def far_kernel(me, pieces, products, others, scale, square):
    rows, count = products.shape
    width = others.shape[1]
    keep = pltpu.with_memory_space_constraint
    return pl.pallas_call(
        functools.partial(far_body, len(pieces), block_of(count, 20)),
        out_shape=(VMEM((rows, count), jnp.float32), VMEM((1, rows), jnp.float32)),
        in_specs=[pl.BlockSpec(memory_space=pltpu.SMEM)] + whole(len(pieces) + 4),
        out_specs=tuple(whole(2)),
        scratch_shapes=[
            VMEM((width, rows), jnp.bfloat16),
            VMEM((rows, width), jnp.bfloat16),
            VMEM((rows, LANES), jnp.float32),
            VMEM((rows, LANES), jnp.float32),
        ],
        input_output_aliases={1 + len(pieces): 0},
        compiler_params=pltpu.CompilerParams(vmem_limit_bytes=32 << 20),
        name="far_kernel",
    )(me, *(keep(p, VMEM) for p in pieces), keep(products, VMEM), keep(others, VMEM), keep(scale, VMEM), keep(square, VMEM))


def added(refs):
    total = refs[0][...]
    for ref in refs[1:]:
        total = total + ref[...]
    return total


def column_body(kernel_ref, *refs):
    *sums, out_ref, spread, part = refs
    spread[...] = to_rows(1.0 / added(sums))
    rows, count = kernel_ref.shape
    group = 64
    part[...] = jnp.zeros_like(part)

    def chunk(i, carry):
        at = pl.ds(pl.multiple_of(i * group, group), group)
        view, scale = kernel_ref.at[at, :], spread[at, :]
        for j in range(0, count, LANES):
            lanes = slice(j, j + LANES)
            value = (view[:, lanes] * scale).reshape(group // 8, 8, LANES)
            part[:, lanes] += jnp.sum(value, axis=0)
        return carry

    lax.fori_loop(0, rows // group, chunk, 0)
    out_ref[...] = jnp.sum(part[...], axis=0, keepdims=True)


def column_sums(kernel, sums):
    rows, count = kernel.shape
    return pl.pallas_call(
        column_body,
        out_shape=jax.ShapeDtypeStruct((1, count), jnp.float32),
        in_specs=whole(1 + len(sums)),
        out_specs=whole(1)[0],
        scratch_shapes=[VMEM((rows, LANES), jnp.float32), VMEM((8, count), jnp.float32)],
        compiler_params=SMALL,
        name="column_sums",
    )(pltpu.with_memory_space_constraint(kernel, VMEM), *sums)


def row_body(kernel_ref, sums_ref, counts_ref, out_ref, scale_ref, part):
    scale_ref[...] = counts_ref[...].astype(jnp.float32) / jnp.sum(sums_ref[...], axis=0)
    rows, count = kernel_ref.shape
    group, block = 64, block_of(count, 8)
    part[...] = jnp.zeros_like(part)

    def chunk(j, carry):
        span = pl.ds(pl.multiple_of(j * block, block), block)
        view, scale = kernel_ref.at[:, span], scale_ref.at[:, span]
        for r in range(0, rows, group):
            at = slice(r, r + group)
            total = part[at, :]
            for k in range(0, block, LANES):
                total = total + view[at, k : k + LANES] * scale[:, k : k + LANES]
            part[at, :] = total
        return carry

    lax.fori_loop(0, count // block, chunk, 0)
    out_ref[...] = to_lanes(part[...])


def row_sums(kernel, sums, counts):
    rows, count = kernel.shape
    return pl.pallas_call(
        row_body,
        out_shape=(
            jax.ShapeDtypeStruct((1, rows), jnp.float32),
            jax.ShapeDtypeStruct((1, count), jnp.float32),
        ),
        in_specs=whole(3),
        out_specs=tuple(whole(2)),
        scratch_shapes=[VMEM((rows, LANES), jnp.float32)],
        compiler_params=SMALL,
        name="row_sums",
    )(pltpu.with_memory_space_constraint(kernel, VMEM), sums, counts)


def assign_body(kernel_ref, scale_ref, *refs):
    *sums, out_ref, spread, ready, sems = refs
    spread[...] = to_rows(1.0 / added(sums))
    stripes, group, count = ready.shape

    def put(i):
        return pltpu.make_async_copy(ready.at[i], out_ref.at[pl.ds(i * group, group), :], sems.at[i])

    def step(i, carry):
        at = pl.ds(pl.multiple_of(i * group, group), group)
        for j in range(count // LANES):
            lanes = slice(j * LANES, (j + 1) * LANES)
            value = spread[at, :] * kernel_ref[at, lanes] * scale_ref[:, lanes]
            ready[i, :, lanes] = value.astype(jnp.bfloat16)
        put(i).start()
        return carry

    lax.fori_loop(0, stripes, step, 0)
    for i in range(stripes):
        put(i).wait()


def assign(kernel, scale, sums):
    rows, count = kernel.shape
    group = 64
    return pl.pallas_call(
        assign_body,
        out_shape=jax.ShapeDtypeStruct((rows, count), jnp.bfloat16),
        in_specs=whole(2 + len(sums)),
        out_specs=pl.BlockSpec(memory_space=pl.ANY),
        scratch_shapes=[
            VMEM((rows, LANES), jnp.float32),
            VMEM((rows // group, group, count), jnp.bfloat16),
            pltpu.SemaphoreType.DMA((rows // group,)),
        ],
        compiler_params=SMALL,
        name="assign",
    )(pltpu.with_memory_space_constraint(kernel, VMEM), scale, *sums)


def gathered(piece, steps):
    held = [piece]
    for bit in steps:
        held = held + [exchange(h, "cls", bit) for h in held]
    return held


def shards(shapes, classes, counts):
    *low, top = bits("cls")
    me = jnp.reshape(lax.axis_index("cls"), (1,)).astype(jnp.int32)
    mine = shapes.T
    other = exchange(mine, "cls", top)
    lhs, rest = near_products(me, gathered(mine, low), classes)
    lhs, other = lax.optimization_barrier((lhs, other))
    pieces = gathered(other, low)
    kernel, sums = far_kernel(me, pieces, *rest(lhs))
    target = counts[None, :]
    for step in range(ITERS):
        columns = spread_out(column_sums(kernel, terms(sums, "cls")), "shape")
        sums, col_scale = row_sums(kernel, columns, target)
    return assign(kernel, col_scale, terms(sums, "cls"))


def solution(mesh):
    placed = (P("shape", "cls"), P("cls", None), P("cls"))
    return jax.shard_map(
        shards, mesh=mesh, in_specs=placed, out_specs=P("shape", "cls"), check_vma=False
    )
```

```python
import functools

import jax
import jax.numpy as jnp
from jax import lax
from jax.experimental import pallas as pl
from jax.experimental.pallas import tpu as pltpu
from jax.sharding import PartitionSpec as P

ITERS = 3

logit_scale = 40.0
epsilon = 1e-06
LANES = 128
VMEM = pltpu.VMEM
SMALL = pltpu.CompilerParams(vmem_limit_bytes=16 << 20)


def bits(axis):
    size = lax.axis_size(axis)
    assert size & (size - 1) == 0
    return [1 << b for b in range(size.bit_length() - 1)]


def exchange(value, axis, bit):
    size = lax.axis_size(axis)
    return lax.ppermute(value, axis, [(i, i ^ bit) for i in range(size)])


def terms(value, axis):
    parts, steps = [value], bits(axis)
    for at in range(0, len(steps), 2):
        value = sum(parts[1:], parts[0])
        offsets = [0]
        for bit in steps[at : at + 2]:
            offsets = offsets + [o ^ bit for o in offsets]
        parts = [value] + [exchange(value, axis, o) for o in offsets[1:]]
    return parts


def spread_out(value, axis):
    copies = jnp.broadcast_to(value[None], (lax.axis_size(axis),) + value.shape)
    return lax.all_to_all(copies, axis, 0, 0)


def whole(count):
    return [pl.BlockSpec(memory_space=VMEM)] * count


def tile(index):
    return pl.ds(pl.multiple_of(index * LANES, LANES), LANES)


def to_lanes(value):
    return jnp.sum(value.T, axis=0, keepdims=True)


def to_rows(value):
    return jnp.broadcast_to(value, (LANES, value.shape[1])).T


def slot(pieces, turned, me, offset):
    depth = turned.shape[0] // pieces
    index = lax.bitwise_and(lax.bitwise_xor(me, offset), pieces - 1)
    return turned.at[pl.ds(pl.multiple_of(index * depth, depth), depth), :]


def place(pieces, turned, me, start=0):
    for offset in range(start, len(pieces)):
        slot(len(pieces), turned, me, offset)[...] = pieces[offset][...]


def squares(value_ref, at=slice(None)):
    total = None
    for t in range(value_ref.shape[1] // LANES):
        value = value_ref[at, t * LANES : (t + 1) * LANES].astype(jnp.float32)
        total = value * value if total is None else total + value * value
    return total


def product(lhs, rhs):
    return lax.dot_general(lhs, rhs, (((1,), (1,)), ((), ())), preferred_element_type=jnp.float32)


def near_body(chunks, block, ahead, me_ref, *refs):
    pieces = refs[:chunks]
    classes_ref, products_ref, others_ref, scale_ref, square_ref, turned, lhs, own, held, sems = refs[chunks:]
    width, blocks = lhs.shape[1], held.shape[0]
    me = me_ref[0]
    mine = lax.div(me, chunks)

    def fetch(i):
        rows = pl.ds(pl.multiple_of(i * block, block), block)
        near = pl.ds(pl.multiple_of(mine * width, LANES), width)
        far = pl.ds(pl.multiple_of((1 - mine) * width, LANES), width)
        return (
            pltpu.make_async_copy(classes_ref.at[rows, near], held.at[i], sems.at[0, i]),
            pltpu.make_async_copy(classes_ref.at[rows, far], others_ref.at[rows, :], sems.at[1, i]),
        )

    first = pltpu.make_async_copy(pieces[0], slot(chunks, turned, me, 0), own)
    first.start()
    for i in range(min(ahead, blocks)):
        for copy in fetch(i):
            copy.start()
    place(pieces, turned, me, 1)
    first.wait()
    lhs[...] = turned[...].T
    square_ref[...] = squares(lhs)

    def step(i, carry):
        @pl.when(i + ahead < blocks)
        def _():
            for copy in fetch(i + ahead):
                copy.start()

        for copy in fetch(i):
            copy.wait()
        rows = pl.ds(pl.multiple_of(i * block, block), block)
        products_ref[:, rows] = product(lhs[...], held[i])
        total = to_lanes(squares(held.at[i]) + squares(others_ref, rows))
        scale_ref[:, rows] = lax.rsqrt(total + epsilon)
        return carry

    lax.fori_loop(0, blocks, step, 0)


def block_of(count, tiles):
    total = count // LANES
    while total % tiles:
        tiles -= 1
    return tiles * LANES


def near_products(me, pieces, classes):
    count, features = classes.shape
    chunks, rows = len(pieces), pieces[0].shape[1]
    width, block = features // 2, block_of(count, 8)
    blocks = count // block
    keep = pltpu.with_memory_space_constraint
    plain = [pl.BlockSpec(memory_space=pltpu.HBM)]
    return pl.pallas_call(
        functools.partial(near_body, chunks, block, 2),
        out_shape=(
            VMEM((rows, count), jnp.float32),
            VMEM((count, width), jnp.bfloat16),
            VMEM((1, count), jnp.float32),
            VMEM((rows, LANES), jnp.float32),
        ),
        in_specs=[pl.BlockSpec(memory_space=pltpu.SMEM)] + plain + whole(chunks - 1) + plain,
        out_specs=tuple(whole(4)),
        scratch_shapes=[
            VMEM((width, rows), jnp.bfloat16),
            VMEM((rows, width), jnp.bfloat16),
            pltpu.SemaphoreType.DMA(()),
            VMEM((blocks, block, width), jnp.bfloat16),
            pltpu.SemaphoreType.DMA((2, blocks)),
        ],
        cost_estimate=pl.CostEstimate(
            flops=2 * rows * count * width, bytes_accessed=2 * count * features, transcendentals=0
        ),
        compiler_params=pltpu.CompilerParams(vmem_limit_bytes=32 << 20),
        name="near_products",
    )(me, keep(pieces[0], pltpu.HBM), *(keep(p, VMEM) for p in pieces[1:]), keep(classes, pltpu.HBM))


def far_body(chunks, block, me_ref, *refs):
    pieces = refs[:chunks]
    products_ref, others_ref, scale_ref, square_ref, kernel_ref, sums_ref, turned, lhs, factor, part = refs[chunks:]
    place(pieces, turned, me_ref[0])
    lhs[...] = turned[...].T
    square = jnp.sum(square_ref[...] + squares(lhs), axis=1, keepdims=True)
    factor[...] = jnp.broadcast_to(logit_scale * lax.rsqrt(square + epsilon), factor.shape)
    part[...] = jnp.zeros_like(part)

    group = 64

    def step(i, carry):
        span = pl.ds(pl.multiple_of(i * block, block), block)
        view, scale = kernel_ref.at[:, span], scale_ref.at[:, span]
        view[...] = products_ref[:, span] + product(lhs[...], others_ref[span, :])
        for r in range(0, part.shape[0], group):
            rows = slice(r, r + group)
            total = part[rows, :]
            for at in range(0, block, LANES):
                lanes = slice(at, at + LANES)
                value = jnp.exp(view[rows, lanes] * factor[rows, :] * scale[:, lanes])
                view[rows, lanes] = value
                total = total + value
            part[rows, :] = total
        return carry

    lax.fori_loop(0, others_ref.shape[0] // block, step, 0)
    sums_ref[...] = to_lanes(part[...])


def far_kernel(me, pieces, products, others, scale, square):
    rows, count = products.shape
    width = others.shape[1]
    keep = pltpu.with_memory_space_constraint
    return pl.pallas_call(
        functools.partial(far_body, len(pieces), block_of(count, 20)),
        out_shape=(VMEM((rows, count), jnp.float32), VMEM((1, rows), jnp.float32)),
        in_specs=[pl.BlockSpec(memory_space=pltpu.SMEM)] + whole(len(pieces) + 4),
        out_specs=tuple(whole(2)),
        scratch_shapes=[
            VMEM((width, rows), jnp.bfloat16),
            VMEM((rows, width), jnp.bfloat16),
            VMEM((rows, LANES), jnp.float32),
            VMEM((rows, LANES), jnp.float32),
        ],
        input_output_aliases={1 + len(pieces): 0},
        compiler_params=pltpu.CompilerParams(vmem_limit_bytes=32 << 20),
        name="far_kernel",
    )(me, *(keep(p, VMEM) for p in pieces), keep(products, VMEM), keep(others, VMEM), keep(scale, VMEM), keep(square, VMEM))


def added(refs):
    total = refs[0][...]
    for ref in refs[1:]:
        total = total + ref[...]
    return total


def column_body(kernel_ref, *refs):
    *sums, out_ref, spread, part = refs
    spread[...] = to_rows(1.0 / added(sums))
    rows, count = kernel_ref.shape
    group = 64
    part[...] = jnp.zeros_like(part)

    def chunk(i, carry):
        at = pl.ds(pl.multiple_of(i * group, group), group)
        view, scale = kernel_ref.at[at, :], spread[at, :]
        for j in range(0, count, LANES):
            lanes = slice(j, j + LANES)
            value = (view[:, lanes] * scale).reshape(group // 8, 8, LANES)
            part[:, lanes] += jnp.sum(value, axis=0)
        return carry

    lax.fori_loop(0, rows // group, chunk, 0)
    out_ref[...] = jnp.sum(part[...], axis=0, keepdims=True)


def column_sums(kernel, sums):
    rows, count = kernel.shape
    return pl.pallas_call(
        column_body,
        out_shape=jax.ShapeDtypeStruct((1, count), jnp.float32),
        in_specs=whole(1 + len(sums)),
        out_specs=whole(1)[0],
        scratch_shapes=[VMEM((rows, LANES), jnp.float32), VMEM((8, count), jnp.float32)],
        compiler_params=SMALL,
        name="column_sums",
    )(pltpu.with_memory_space_constraint(kernel, VMEM), *sums)


def row_body(kernel_ref, sums_ref, counts_ref, out_ref, scale_ref, part):
    scale_ref[...] = counts_ref[...].astype(jnp.float32) / jnp.sum(sums_ref[...], axis=0)
    rows, count = kernel_ref.shape
    group, block = 64, block_of(count, 8)
    part[...] = jnp.zeros_like(part)

    def chunk(j, carry):
        span = pl.ds(pl.multiple_of(j * block, block), block)
        view, scale = kernel_ref.at[:, span], scale_ref.at[:, span]
        for r in range(0, rows, group):
            at = slice(r, r + group)
            total = part[at, :]
            for k in range(0, block, LANES):
                total = total + view[at, k : k + LANES] * scale[:, k : k + LANES]
            part[at, :] = total
        return carry

    lax.fori_loop(0, count // block, chunk, 0)
    out_ref[...] = to_lanes(part[...])


def row_sums(kernel, sums, counts):
    rows, count = kernel.shape
    return pl.pallas_call(
        row_body,
        out_shape=(
            jax.ShapeDtypeStruct((1, rows), jnp.float32),
            jax.ShapeDtypeStruct((1, count), jnp.float32),
        ),
        in_specs=whole(3),
        out_specs=tuple(whole(2)),
        scratch_shapes=[VMEM((rows, LANES), jnp.float32)],
        compiler_params=SMALL,
        name="row_sums",
    )(pltpu.with_memory_space_constraint(kernel, VMEM), sums, counts)


def assign_body(kernel_ref, scale_ref, *refs):
    *sums, out_ref, spread, ready, sems = refs
    spread[...] = to_rows(1.0 / added(sums))
    stripes, group, count = ready.shape

    def put(i):
        return pltpu.make_async_copy(ready.at[i], out_ref.at[pl.ds(i * group, group), :], sems.at[i])

    def step(i, carry):
        at = pl.ds(pl.multiple_of(i * group, group), group)
        for j in range(count // LANES):
            lanes = slice(j * LANES, (j + 1) * LANES)
            value = spread[at, :] * kernel_ref[at, lanes] * scale_ref[:, lanes]
            ready[i, :, lanes] = value.astype(jnp.bfloat16)
        put(i).start()
        return carry

    lax.fori_loop(0, stripes, step, 0)
    for i in range(stripes):
        put(i).wait()


def assign(kernel, scale, sums):
    rows, count = kernel.shape
    group = 64
    return pl.pallas_call(
        assign_body,
        out_shape=jax.ShapeDtypeStruct((rows, count), jnp.bfloat16),
        in_specs=whole(2 + len(sums)),
        out_specs=pl.BlockSpec(memory_space=pl.ANY),
        scratch_shapes=[
            VMEM((rows, LANES), jnp.float32),
            VMEM((rows // group, group, count), jnp.bfloat16),
            pltpu.SemaphoreType.DMA((rows // group,)),
        ],
        compiler_params=SMALL,
        name="assign",
    )(pltpu.with_memory_space_constraint(kernel, VMEM), scale, *sums)


def gathered(piece, steps):
    held = [piece]
    for bit in steps:
        held = held + [exchange(h, "cls", bit) for h in held]
    return held


def shards(shapes, classes, counts):
    *low, top = bits("cls")
    me = jnp.reshape(lax.axis_index("cls"), (1,)).astype(jnp.int32)
    mine = shapes.T
    other = exchange(mine, "cls", top)
    *near, square = near_products(me, gathered(mine, low), classes)
    square, other = lax.optimization_barrier((square, other))
    kernel, sums = far_kernel(me, gathered(other, low), *near, square)
    target = counts[None, :]
    for step in range(ITERS):
        columns = spread_out(column_sums(kernel, terms(sums, "cls")), "shape")
        sums, col_scale = row_sums(kernel, columns, target)
    return assign(kernel, col_scale, terms(sums, "cls"))


def solution(mesh):
    placed = (P("shape", "cls"), P("cls", None), P("cls"))
    return jax.shard_map(
        shards, mesh=mesh, in_specs=placed, out_specs=P("shape", "cls"), check_vma=False
    )
```

```python
import functools

import jax
import jax.numpy as jnp
from jax import lax
from jax.experimental import pallas as pl
from jax.experimental.pallas import tpu as pltpu
from jax.sharding import PartitionSpec as P

ITERS = 3

logit_scale = 40.0
epsilon = 1e-06
LANES = 128
VMEM = pltpu.VMEM
SMALL = pltpu.CompilerParams(vmem_limit_bytes=16 << 20)


def bits(axis):
    size = lax.axis_size(axis)
    assert size & (size - 1) == 0
    return [1 << b for b in range(size.bit_length() - 1)]


def exchange(value, axis, bit):
    size = lax.axis_size(axis)
    return lax.ppermute(value, axis, [(i, i ^ bit) for i in range(size)])


def terms(value, axis):
    parts, steps = [value], bits(axis)
    for at in range(0, len(steps), 2):
        value = sum(parts[1:], parts[0])
        offsets = [0]
        for bit in steps[at : at + 2]:
            offsets = offsets + [o ^ bit for o in offsets]
        parts = [value] + [exchange(value, axis, o) for o in offsets[1:]]
    return parts


def whole(count):
    return [pl.BlockSpec(memory_space=VMEM)] * count


def tile(index):
    return pl.ds(pl.multiple_of(index * LANES, LANES), LANES)


def to_lanes(value):
    return jnp.sum(value.T, axis=0, keepdims=True)


def to_rows(value):
    return jnp.broadcast_to(value, (LANES, value.shape[1])).T


def slot(pieces, turned, me, offset):
    depth = turned.shape[0] // pieces
    index = lax.bitwise_and(lax.bitwise_xor(me, offset), pieces - 1)
    return turned.at[pl.ds(pl.multiple_of(index * depth, depth), depth), :]


def place(pieces, turned, me, start=0):
    for offset in range(start, len(pieces)):
        slot(len(pieces), turned, me, offset)[...] = pieces[offset][...]


def squares(value_ref, at=slice(None)):
    total = None
    for t in range(value_ref.shape[1] // LANES):
        value = value_ref[at, t * LANES : (t + 1) * LANES].astype(jnp.float32)
        total = value * value if total is None else total + value * value
    return total


def product(lhs, rhs):
    return lax.dot_general(lhs, rhs, (((1,), (1,)), ((), ())), preferred_element_type=jnp.float32)


def near_body(chunks, block, ahead, me_ref, *refs):
    pieces = refs[:chunks]
    classes_ref, products_ref, others_ref, scale_ref, square_ref, turned, lhs, own, held, sems = refs[chunks:]
    width, blocks = lhs.shape[1], held.shape[0]
    me = me_ref[0]
    mine = lax.div(me, chunks)

    def fetch(i):
        rows = pl.ds(pl.multiple_of(i * block, block), block)
        near = pl.ds(pl.multiple_of(mine * width, LANES), width)
        far = pl.ds(pl.multiple_of((1 - mine) * width, LANES), width)
        return (
            pltpu.make_async_copy(classes_ref.at[rows, near], held.at[i], sems.at[0, i]),
            pltpu.make_async_copy(classes_ref.at[rows, far], others_ref.at[rows, :], sems.at[1, i]),
        )

    first = pltpu.make_async_copy(pieces[0], slot(chunks, turned, me, 0), own)
    first.start()
    for i in range(min(ahead, blocks)):
        for copy in fetch(i):
            copy.start()
    place(pieces, turned, me, 1)
    first.wait()
    lhs[...] = turned[...].T
    square_ref[...] = squares(lhs)

    def step(i, carry):
        @pl.when(i + ahead < blocks)
        def _():
            for copy in fetch(i + ahead):
                copy.start()

        for copy in fetch(i):
            copy.wait()
        rows = pl.ds(pl.multiple_of(i * block, block), block)
        products_ref[:, rows] = product(lhs[...], held[i])
        total = to_lanes(squares(held.at[i]) + squares(others_ref, rows))
        scale_ref[:, rows] = lax.rsqrt(total + epsilon)
        return carry

    lax.fori_loop(0, blocks, step, 0)


def block_of(count, tiles):
    total = count // LANES
    while total % tiles:
        tiles -= 1
    return tiles * LANES


def near_products(me, pieces, classes):
    count, features = classes.shape
    chunks, rows = len(pieces), pieces[0].shape[1]
    width, block = features // 2, block_of(count, 8)
    blocks = count // block
    keep = pltpu.with_memory_space_constraint
    plain = [pl.BlockSpec(memory_space=pltpu.HBM)]
    return pl.pallas_call(
        functools.partial(near_body, chunks, block, 2),
        out_shape=(
            VMEM((rows, count), jnp.float32),
            VMEM((count, width), jnp.bfloat16),
            VMEM((1, count), jnp.float32),
            VMEM((rows, LANES), jnp.float32),
        ),
        in_specs=[pl.BlockSpec(memory_space=pltpu.SMEM)] + plain + whole(chunks - 1) + plain,
        out_specs=tuple(whole(4)),
        scratch_shapes=[
            VMEM((width, rows), jnp.bfloat16),
            VMEM((rows, width), jnp.bfloat16),
            pltpu.SemaphoreType.DMA(()),
            VMEM((blocks, block, width), jnp.bfloat16),
            pltpu.SemaphoreType.DMA((2, blocks)),
        ],
        cost_estimate=pl.CostEstimate(
            flops=2 * rows * count * width, bytes_accessed=2 * count * features, transcendentals=0
        ),
        compiler_params=pltpu.CompilerParams(vmem_limit_bytes=32 << 20),
        name="near_products",
    )(me, keep(pieces[0], pltpu.HBM), *(keep(p, VMEM) for p in pieces[1:]), keep(classes, pltpu.HBM))


def far_body(chunks, block, me_ref, *refs):
    pieces = refs[:chunks]
    products_ref, others_ref, scale_ref, square_ref, kernel_ref, sums_ref, turned, lhs, factor, part = refs[chunks:]
    place(pieces, turned, me_ref[0])
    lhs[...] = turned[...].T
    square = jnp.sum(square_ref[...] + squares(lhs), axis=1, keepdims=True)
    factor[...] = jnp.broadcast_to(logit_scale * lax.rsqrt(square + epsilon), factor.shape)
    part[...] = jnp.zeros_like(part)

    group = 64

    def step(i, carry):
        span = pl.ds(pl.multiple_of(i * block, block), block)
        view, scale = kernel_ref.at[:, span], scale_ref.at[:, span]
        view[...] = products_ref[:, span] + product(lhs[...], others_ref[span, :])
        for r in range(0, part.shape[0], group):
            rows = slice(r, r + group)
            total = part[rows, :]
            for at in range(0, block, LANES):
                lanes = slice(at, at + LANES)
                value = jnp.exp(view[rows, lanes] * factor[rows, :] * scale[:, lanes])
                view[rows, lanes] = value
                total = total + value
            part[rows, :] = total
        return carry

    lax.fori_loop(0, others_ref.shape[0] // block, step, 0)
    sums_ref[...] = to_lanes(part[...])


def far_kernel(me, pieces, products, others, scale, square):
    rows, count = products.shape
    width = others.shape[1]
    keep = pltpu.with_memory_space_constraint
    return pl.pallas_call(
        functools.partial(far_body, len(pieces), block_of(count, 20)),
        out_shape=(VMEM((rows, count), jnp.float32), VMEM((1, rows), jnp.float32)),
        in_specs=[pl.BlockSpec(memory_space=pltpu.SMEM)] + whole(len(pieces) + 4),
        out_specs=tuple(whole(2)),
        scratch_shapes=[
            VMEM((width, rows), jnp.bfloat16),
            VMEM((rows, width), jnp.bfloat16),
            VMEM((rows, LANES), jnp.float32),
            VMEM((rows, LANES), jnp.float32),
        ],
        input_output_aliases={1 + len(pieces): 0},
        compiler_params=pltpu.CompilerParams(vmem_limit_bytes=32 << 20),
        name="far_kernel",
    )(me, *(keep(p, VMEM) for p in pieces), keep(products, VMEM), keep(others, VMEM), keep(scale, VMEM), keep(square, VMEM))


def added(refs):
    total = refs[0][...]
    for ref in refs[1:]:
        total = total + ref[...]
    return total


def column_body(kernel_ref, *refs):
    *sums, out_ref, spread, part = refs
    spread[...] = to_rows(1.0 / added(sums))
    rows, count = kernel_ref.shape
    group = 64
    part[...] = jnp.zeros_like(part)

    def chunk(i, carry):
        at = pl.ds(pl.multiple_of(i * group, group), group)
        view, scale = kernel_ref.at[at, :], spread[at, :]
        for j in range(0, count, LANES):
            lanes = slice(j, j + LANES)
            value = (view[:, lanes] * scale).reshape(group // 8, 8, LANES)
            part[:, lanes] += jnp.sum(value, axis=0)
        return carry

    lax.fori_loop(0, rows // group, chunk, 0)
    total = jnp.sum(part[...], axis=0, keepdims=True)
    out_ref[...] = jnp.broadcast_to(total[None], out_ref.shape)


def column_sums(kernel, sums, copies):
    rows, count = kernel.shape
    return pl.pallas_call(
        column_body,
        out_shape=VMEM((copies, 1, count), jnp.float32),
        in_specs=whole(1 + len(sums)),
        out_specs=whole(1)[0],
        scratch_shapes=[VMEM((rows, LANES), jnp.float32), VMEM((8, count), jnp.float32)],
        compiler_params=SMALL,
        name="column_sums",
    )(pltpu.with_memory_space_constraint(kernel, VMEM), *sums)


def row_body(kernel_ref, sums_ref, counts_ref, out_ref, scale_ref, part):
    scale_ref[...] = counts_ref[...].astype(jnp.float32) / jnp.sum(sums_ref[...], axis=0)
    rows, count = kernel_ref.shape
    group, block = 64, block_of(count, 8)
    part[...] = jnp.zeros_like(part)

    def chunk(j, carry):
        span = pl.ds(pl.multiple_of(j * block, block), block)
        view, scale = kernel_ref.at[:, span], scale_ref.at[:, span]
        for r in range(0, rows, group):
            at = slice(r, r + group)
            total = part[at, :]
            for k in range(0, block, LANES):
                total = total + view[at, k : k + LANES] * scale[:, k : k + LANES]
            part[at, :] = total
        return carry

    lax.fori_loop(0, count // block, chunk, 0)
    out_ref[...] = to_lanes(part[...])


def row_sums(kernel, sums, counts, last):
    rows, count = kernel.shape
    outputs = (VMEM((1, rows), jnp.float32), VMEM((1, count), jnp.float32))
    result = pl.pallas_call(
        row_body,
        out_shape=outputs[: 1 + last],
        in_specs=whole(3),
        out_specs=tuple(whole(1 + last)),
        scratch_shapes=[*outputs[1 + last :], VMEM((rows, LANES), jnp.float32)],
        compiler_params=SMALL,
        name="row_sums",
    )(pltpu.with_memory_space_constraint(kernel, VMEM), sums, counts)
    return result if last else (*result, None)


def assign_body(kernel_ref, scale_ref, *refs):
    *sums, out_ref, spread, ready, sems = refs
    spread[...] = to_rows(1.0 / added(sums))
    stripes, group, count = ready.shape

    def put(i):
        return pltpu.make_async_copy(ready.at[i], out_ref.at[pl.ds(i * group, group), :], sems.at[i])

    def step(i, carry):
        at = pl.ds(pl.multiple_of(i * group, group), group)
        for j in range(count // LANES):
            lanes = slice(j * LANES, (j + 1) * LANES)
            value = spread[at, :] * kernel_ref[at, lanes] * scale_ref[:, lanes]
            ready[i, :, lanes] = value.astype(jnp.bfloat16)
        put(i).start()
        return carry

    lax.fori_loop(0, stripes, step, 0)
    for i in range(stripes):
        put(i).wait()


def assign(kernel, scale, sums):
    rows, count = kernel.shape
    group = 64
    return pl.pallas_call(
        assign_body,
        out_shape=jax.ShapeDtypeStruct((rows, count), jnp.bfloat16),
        in_specs=whole(2 + len(sums)),
        out_specs=pl.BlockSpec(memory_space=pl.ANY),
        scratch_shapes=[
            VMEM((rows, LANES), jnp.float32),
            VMEM((rows // group, group, count), jnp.bfloat16),
            pltpu.SemaphoreType.DMA((rows // group,)),
        ],
        compiler_params=SMALL,
        name="assign",
    )(pltpu.with_memory_space_constraint(kernel, VMEM), scale, *sums)


def gathered(piece, steps):
    held = [piece]
    for bit in steps:
        held = held + [exchange(h, "cls", bit) for h in held]
    return held


def shards(shapes, classes, counts):
    *low, top = bits("cls")
    me = jnp.reshape(lax.axis_index("cls"), (1,)).astype(jnp.int32)
    mine = shapes.T
    other = exchange(mine, "cls", top)
    *near, square = near_products(me, gathered(mine, low), classes)
    square, other = lax.optimization_barrier((square, other))
    kernel, sums = far_kernel(me, gathered(other, low), *near, square)
    target = counts[None, :]
    for step in range(ITERS):
        copies = column_sums(kernel, terms(sums, "cls"), lax.axis_size("shape"))
        columns = lax.all_to_all(copies, "shape", 0, 0)
        sums, col_scale = row_sums(kernel, columns, target, step == ITERS - 1)
    return assign(kernel, col_scale, terms(sums, "cls"))


def solution(mesh):
    placed = (P("shape", "cls"), P("cls", None), P("cls"))
    return jax.shard_map(
        shards, mesh=mesh, in_specs=placed, out_specs=P("shape", "cls"), check_vma=False
    )
```

```python
import functools

import jax
import jax.numpy as jnp
from jax import lax
from jax.experimental import pallas as pl
from jax.experimental.pallas import tpu as pltpu
from jax.sharding import PartitionSpec as P

ITERS = 3

logit_scale = 40.0
epsilon = 1e-06
LANES = 128
VMEM = pltpu.VMEM
SMALL = pltpu.CompilerParams(vmem_limit_bytes=16 << 20)


def bits(axis):
    size = lax.axis_size(axis)
    assert size & (size - 1) == 0
    return [1 << b for b in range(size.bit_length() - 1)]


def exchange(value, axis, bit):
    size = lax.axis_size(axis)
    return lax.ppermute(value, axis, [(i, i ^ bit) for i in range(size)])


def terms(value, axis):
    parts, steps = [value], bits(axis)
    for at in range(0, len(steps), 2):
        value = sum(parts[1:], parts[0])
        offsets = [0]
        for bit in steps[at : at + 2]:
            offsets = offsets + [o ^ bit for o in offsets]
        parts = [value] + [exchange(value, axis, o) for o in offsets[1:]]
    return parts


def whole(count):
    return [pl.BlockSpec(memory_space=VMEM)] * count


def tile(index):
    return pl.ds(pl.multiple_of(index * LANES, LANES), LANES)


def to_lanes(value):
    return jnp.sum(value.T, axis=0, keepdims=True)


def to_rows(value):
    return jnp.broadcast_to(value, (LANES, value.shape[1])).T


def slot(pieces, turned, me, offset):
    depth = turned.shape[0] // pieces
    index = lax.bitwise_and(lax.bitwise_xor(me, offset), pieces - 1)
    return turned.at[pl.ds(pl.multiple_of(index * depth, depth), depth), :]


def place(pieces, turned, me, start=0):
    for offset in range(start, len(pieces)):
        slot(len(pieces), turned, me, offset)[...] = pieces[offset][...]


def squares(value_ref, at=slice(None)):
    total = None
    for t in range(value_ref.shape[1] // LANES):
        value = value_ref[at, t * LANES : (t + 1) * LANES].astype(jnp.float32)
        total = value * value if total is None else total + value * value
    return total


def product(lhs, rhs):
    return lax.dot_general(lhs, rhs, (((1,), (1,)), ((), ())), preferred_element_type=jnp.float32)


def near_body(chunks, block, ahead, me_ref, *refs):
    pieces = refs[:chunks]
    classes_ref, products_ref, others_ref, scale_ref, square_ref, turned, lhs, own, held, sems = refs[chunks:]
    width, blocks = lhs.shape[1], held.shape[0]
    me = me_ref[0]
    mine = lax.div(me, chunks)

    def fetch(i):
        rows = pl.ds(pl.multiple_of(i * block, block), block)
        near = pl.ds(pl.multiple_of(mine * width, LANES), width)
        far = pl.ds(pl.multiple_of((1 - mine) * width, LANES), width)
        return (
            pltpu.make_async_copy(classes_ref.at[rows, near], held.at[i], sems.at[0, i]),
            pltpu.make_async_copy(classes_ref.at[rows, far], others_ref.at[rows, :], sems.at[1, i]),
        )

    first = pltpu.make_async_copy(pieces[0], slot(chunks, turned, me, 0), own)
    first.start()
    for i in range(min(ahead, blocks)):
        for copy in fetch(i):
            copy.start()
    place(pieces, turned, me, 1)
    first.wait()
    lhs[...] = turned[...].T
    square_ref[...] = squares(lhs)

    def step(i, carry):
        @pl.when(i + ahead < blocks)
        def _():
            for copy in fetch(i + ahead):
                copy.start()

        for copy in fetch(i):
            copy.wait()
        rows = pl.ds(pl.multiple_of(i * block, block), block)
        products_ref[:, rows] = product(lhs[...], held[i])
        total = to_lanes(squares(held.at[i]) + squares(others_ref, rows))
        scale_ref[:, rows] = lax.rsqrt(total + epsilon)
        return carry

    lax.fori_loop(0, blocks, step, 0)


def block_of(count, tiles):
    total = count // LANES
    while total % tiles:
        tiles -= 1
    return tiles * LANES


def near_products(me, pieces, classes):
    count, features = classes.shape
    chunks, rows = len(pieces), pieces[0].shape[1]
    width, block = features // 2, block_of(count, 8)
    blocks = count // block
    keep = pltpu.with_memory_space_constraint
    plain = [pl.BlockSpec(memory_space=pltpu.HBM)]
    return pl.pallas_call(
        functools.partial(near_body, chunks, block, 2),
        out_shape=(
            VMEM((rows, count), jnp.float32),
            VMEM((count, width), jnp.bfloat16),
            VMEM((1, count), jnp.float32),
            VMEM((rows, LANES), jnp.float32),
        ),
        in_specs=[pl.BlockSpec(memory_space=pltpu.SMEM)] + plain + whole(chunks - 1) + plain,
        out_specs=tuple(whole(4)),
        scratch_shapes=[
            VMEM((width, rows), jnp.bfloat16),
            VMEM((rows, width), jnp.bfloat16),
            pltpu.SemaphoreType.DMA(()),
            VMEM((blocks, block, width), jnp.bfloat16),
            pltpu.SemaphoreType.DMA((2, blocks)),
        ],
        cost_estimate=pl.CostEstimate(
            flops=2 * rows * count * width, bytes_accessed=2 * count * features, transcendentals=0
        ),
        compiler_params=pltpu.CompilerParams(vmem_limit_bytes=32 << 20),
        name="near_products",
    )(me, keep(pieces[0], pltpu.HBM), *(keep(p, VMEM) for p in pieces[1:]), keep(classes, pltpu.HBM))


def early_width(pieces, depth):
    return depth // 256 * 256 if pieces == 2 else 0


def early_body(early, me_ref, piece, products_ref, others_ref, square_ref, sums_ref, total_ref, lhs):
    depth, width = piece.shape[0], others_ref.shape[1]
    index = lax.rem(me_ref[0], 2)
    lhs[...] = piece[pl.ds(pl.multiple_of(index * (depth - early), 16), early), :].T
    total_ref[...] = square_ref[...] + squares(lhs)
    lanes = pl.ds(pl.multiple_of(index * (width - early), LANES), early)
    sums_ref[...] = products_ref[...] + product(lhs[...], others_ref[:, lanes])


def early_products(early, me, piece, products, others, square):
    rows, count = products.shape
    keep = pltpu.with_memory_space_constraint
    return pl.pallas_call(
        functools.partial(early_body, early),
        out_shape=(VMEM((rows, count), jnp.float32), VMEM((rows, LANES), jnp.float32)),
        in_specs=[pl.BlockSpec(memory_space=pltpu.SMEM)] + whole(4),
        out_specs=tuple(whole(2)),
        scratch_shapes=[VMEM((rows, early), jnp.bfloat16)],
        input_output_aliases={2: 0},
        cost_estimate=pl.CostEstimate(
            flops=2 * rows * count * early, bytes_accessed=8 * rows * count, transcendentals=0
        ),
        compiler_params=pltpu.CompilerParams(vmem_limit_bytes=24 << 20),
        name="early_products",
    )(me, keep(piece, VMEM), keep(products, VMEM), keep(others, VMEM), keep(square, VMEM))


def far_body(chunks, block, early, me_ref, *refs):
    pieces = refs[:chunks]
    products_ref, others_ref, scale_ref, square_ref, kernel_ref, sums_ref, turned, lhs, factor, part = refs[chunks:]
    place(pieces, turned, me_ref[0])
    start = pl.multiple_of(early - lax.rem(me_ref[0], 2) * early, LANES)
    lhs[...] = turned[pl.ds(start, lhs.shape[1]), :].T
    square = jnp.sum(square_ref[...] + squares(lhs), axis=1, keepdims=True)
    factor[...] = jnp.broadcast_to(logit_scale * lax.rsqrt(square + epsilon), factor.shape)
    part[...] = jnp.zeros_like(part)

    group = 64

    def step(i, carry):
        span = pl.ds(pl.multiple_of(i * block, block), block)
        view, scale = kernel_ref.at[:, span], scale_ref.at[:, span]
        view[...] = products_ref[:, span] + product(lhs[...], others_ref[span, pl.ds(start, lhs.shape[1])])
        for r in range(0, part.shape[0], group):
            rows = slice(r, r + group)
            total = part[rows, :]
            for at in range(0, block, LANES):
                lanes = slice(at, at + LANES)
                value = jnp.exp(view[rows, lanes] * factor[rows, :] * scale[:, lanes])
                view[rows, lanes] = value
                total = total + value
            part[rows, :] = total
        return carry

    lax.fori_loop(0, others_ref.shape[0] // block, step, 0)
    sums_ref[...] = to_lanes(part[...])


def far_kernel(early, me, pieces, products, others, scale, square):
    rows, count = products.shape
    width = others.shape[1]
    keep = pltpu.with_memory_space_constraint
    return pl.pallas_call(
        functools.partial(far_body, len(pieces), block_of(count, 20), early),
        out_shape=(VMEM((rows, count), jnp.float32), VMEM((1, rows), jnp.float32)),
        in_specs=[pl.BlockSpec(memory_space=pltpu.SMEM)] + whole(len(pieces) + 4),
        out_specs=tuple(whole(2)),
        scratch_shapes=[
            VMEM((width, rows), jnp.bfloat16),
            VMEM((rows, width - early), jnp.bfloat16),
            VMEM((rows, LANES), jnp.float32),
            VMEM((rows, LANES), jnp.float32),
        ],
        input_output_aliases={1 + len(pieces): 0},
        compiler_params=pltpu.CompilerParams(vmem_limit_bytes=32 << 20),
        name="far_kernel",
    )(me, *(keep(p, VMEM) for p in pieces), keep(products, VMEM), keep(others, VMEM), keep(scale, VMEM), keep(square, VMEM))


def added(refs):
    total = refs[0][...]
    for ref in refs[1:]:
        total = total + ref[...]
    return total


def column_body(kernel_ref, *refs):
    *sums, out_ref, spread, part = refs
    spread[...] = to_rows(1.0 / added(sums))
    rows, count = kernel_ref.shape
    group = 64
    part[...] = jnp.zeros_like(part)

    def chunk(i, carry):
        at = pl.ds(pl.multiple_of(i * group, group), group)
        view, scale = kernel_ref.at[at, :], spread[at, :]
        for j in range(0, count, LANES):
            lanes = slice(j, j + LANES)
            value = (view[:, lanes] * scale).reshape(group // 8, 8, LANES)
            part[:, lanes] += jnp.sum(value, axis=0)
        return carry

    lax.fori_loop(0, rows // group, chunk, 0)
    total = jnp.sum(part[...], axis=0, keepdims=True)
    out_ref[...] = jnp.broadcast_to(total[None], out_ref.shape)


def column_sums(kernel, sums, copies):
    rows, count = kernel.shape
    return pl.pallas_call(
        column_body,
        out_shape=VMEM((copies, 1, count), jnp.float32),
        in_specs=whole(1 + len(sums)),
        out_specs=whole(1)[0],
        scratch_shapes=[VMEM((rows, LANES), jnp.float32), VMEM((8, count), jnp.float32)],
        compiler_params=SMALL,
        name="column_sums",
    )(pltpu.with_memory_space_constraint(kernel, VMEM), *sums)


def row_body(kernel_ref, sums_ref, counts_ref, out_ref, scale_ref, part):
    scale_ref[...] = counts_ref[...].astype(jnp.float32) / jnp.sum(sums_ref[...], axis=0)
    rows, count = kernel_ref.shape
    group, block = 64, block_of(count, 8)
    part[...] = jnp.zeros_like(part)

    def chunk(j, carry):
        span = pl.ds(pl.multiple_of(j * block, block), block)
        view, scale = kernel_ref.at[:, span], scale_ref.at[:, span]
        for r in range(0, rows, group):
            at = slice(r, r + group)
            total = part[at, :]
            for k in range(0, block, LANES):
                total = total + view[at, k : k + LANES] * scale[:, k : k + LANES]
            part[at, :] = total
        return carry

    lax.fori_loop(0, count // block, chunk, 0)
    out_ref[...] = to_lanes(part[...])


def row_sums(kernel, sums, counts, last):
    rows, count = kernel.shape
    outputs = (VMEM((1, rows), jnp.float32), VMEM((1, count), jnp.float32))
    result = pl.pallas_call(
        row_body,
        out_shape=outputs[: 1 + last],
        in_specs=whole(3),
        out_specs=tuple(whole(1 + last)),
        scratch_shapes=[*outputs[1 + last :], VMEM((rows, LANES), jnp.float32)],
        compiler_params=SMALL,
        name="row_sums",
    )(pltpu.with_memory_space_constraint(kernel, VMEM), sums, counts)
    return result if last else (*result, None)


def assign_body(kernel_ref, scale_ref, *refs):
    *sums, out_ref, spread, ready, sems = refs
    spread[...] = to_rows(1.0 / added(sums))
    stripes, group, count = ready.shape

    def put(i):
        return pltpu.make_async_copy(ready.at[i], out_ref.at[pl.ds(i * group, group), :], sems.at[i])

    def step(i, carry):
        at = pl.ds(pl.multiple_of(i * group, group), group)
        for j in range(count // LANES):
            lanes = slice(j * LANES, (j + 1) * LANES)
            value = spread[at, :] * kernel_ref[at, lanes] * scale_ref[:, lanes]
            ready[i, :, lanes] = value.astype(jnp.bfloat16)
        put(i).start()
        return carry

    lax.fori_loop(0, stripes, step, 0)
    for i in range(stripes):
        put(i).wait()


def assign(kernel, scale, sums):
    rows, count = kernel.shape
    group = 64
    return pl.pallas_call(
        assign_body,
        out_shape=jax.ShapeDtypeStruct((rows, count), jnp.bfloat16),
        in_specs=whole(2 + len(sums)),
        out_specs=pl.BlockSpec(memory_space=pl.ANY),
        scratch_shapes=[
            VMEM((rows, LANES), jnp.float32),
            VMEM((rows // group, group, count), jnp.bfloat16),
            pltpu.SemaphoreType.DMA((rows // group,)),
        ],
        compiler_params=SMALL,
        name="assign",
    )(pltpu.with_memory_space_constraint(kernel, VMEM), scale, *sums)


def gathered(piece, steps):
    held = [piece]
    for bit in steps:
        held = held + [exchange(h, "cls", bit) for h in held]
    return held


def shards(shapes, classes, counts):
    *low, top = bits("cls")
    me = jnp.reshape(lax.axis_index("cls"), (1,)).astype(jnp.int32)
    mine = shapes.T
    other = exchange(mine, "cls", top)
    products, others, scale, square = near_products(me, gathered(mine, low), classes)
    square, other = lax.optimization_barrier((square, other))
    pieces = gathered(other, low)
    early = early_width(len(pieces), mine.shape[0])
    if early:
        products, square = early_products(early, me, other, products, others, square)
    kernel, sums = far_kernel(early, me, pieces, products, others, scale, square)
    target = counts[None, :]
    for step in range(ITERS):
        copies = column_sums(kernel, terms(sums, "cls"), lax.axis_size("shape"))
        columns = lax.all_to_all(copies, "shape", 0, 0)
        sums, col_scale = row_sums(kernel, columns, target, step == ITERS - 1)
    return assign(kernel, col_scale, terms(sums, "cls"))


def solution(mesh):
    placed = (P("shape", "cls"), P("cls", None), P("cls"))
    return jax.shard_map(
        shards, mesh=mesh, in_specs=placed, out_specs=P("shape", "cls"), check_vma=False
    )
```

```python
import functools

import jax
import jax.numpy as jnp
from jax import lax
from jax.experimental import pallas as pl
from jax.experimental.pallas import tpu as pltpu
from jax.sharding import PartitionSpec as P

ITERS = 3

logit_scale = 40.0
epsilon = 1e-06
LANES = 128
VMEM = pltpu.VMEM
SMALL = pltpu.CompilerParams(vmem_limit_bytes=16 << 20)


def bits(axis):
    size = lax.axis_size(axis)
    assert size & (size - 1) == 0
    return [1 << b for b in range(size.bit_length() - 1)]


def exchange(value, axis, bit):
    size = lax.axis_size(axis)
    return lax.ppermute(value, axis, [(i, i ^ bit) for i in range(size)])


def terms(value, axis):
    parts, steps = [value], bits(axis)
    for at in range(0, len(steps), 2):
        value = sum(parts[1:], parts[0])
        offsets = [0]
        for bit in steps[at : at + 2]:
            offsets = offsets + [o ^ bit for o in offsets]
        parts = [value] + [exchange(value, axis, o) for o in offsets[1:]]
    return parts


def whole(count):
    return [pl.BlockSpec(memory_space=VMEM)] * count


def tile(index):
    return pl.ds(pl.multiple_of(index * LANES, LANES), LANES)


def to_lanes(value):
    return jnp.sum(value.T, axis=0, keepdims=True)


def to_rows(value):
    return jnp.broadcast_to(value, (LANES, value.shape[1])).T


def slot(pieces, turned, me, offset):
    depth = turned.shape[0] // pieces
    index = lax.bitwise_and(lax.bitwise_xor(me, offset), pieces - 1)
    return turned.at[pl.ds(pl.multiple_of(index * depth, depth), depth), :]


def place(pieces, turned, me):
    for offset in range(len(pieces)):
        slot(len(pieces), turned, me, offset)[...] = pieces[offset][...]


def squares(value_ref, at=slice(None)):
    total = None
    for t in range(value_ref.shape[1] // LANES):
        value = value_ref[at, t * LANES : (t + 1) * LANES].astype(jnp.float32)
        total = value * value if total is None else total + value * value
    return total


def product(lhs, rhs):
    return lax.dot_general(lhs, rhs, (((1,), (1,)), ((), ())), preferred_element_type=jnp.float32)


def fetcher(mine, block, width, classes_ref, held, others_ref, sems):
    def fetch(i):
        rows = pl.ds(pl.multiple_of(i * block, block), block)
        near = pl.ds(pl.multiple_of(mine * width, LANES), width)
        far = pl.ds(pl.multiple_of((1 - mine) * width, LANES), width)
        return (
            pltpu.make_async_copy(classes_ref.at[rows, near], held.at[rows, :], sems.at[0, i]),
            pltpu.make_async_copy(classes_ref.at[rows, far], others_ref.at[rows, :], sems.at[1, i]),
        )

    return fetch


def load_body(chunks, block, me_ref, piece, classes_ref, own_ref, held, others_ref, sem, sems):
    fetch = fetcher(lax.div(me_ref[0], chunks), block, held.shape[1], classes_ref, held, others_ref, sems)
    copies = (pltpu.make_async_copy(piece, own_ref, sem), *fetch(0))
    for copy in copies:
        copy.start()
    for copy in copies:
        copy.wait()


def near_body(chunks, block, me_ref, *refs):
    pieces = refs[:chunks]
    classes_ref, _, _, products_ref, held, others_ref, scale_ref, square_ref, turned, lhs, sems = refs[chunks:]
    width, blocks = lhs.shape[1], held.shape[0] // block
    me = me_ref[0]
    fetch = fetcher(lax.div(me, chunks), block, width, classes_ref, held, others_ref, sems)

    for i in range(1, min(3, blocks)):
        for copy in fetch(i):
            copy.start()
    place(pieces, turned, me)
    lhs[...] = turned[...].T
    square_ref[...] = squares(lhs)

    def step(i, carry):
        @pl.when(i > 0)
        def _():
            for copy in fetch(i):
                copy.wait()

        @pl.when((i > 0) & (i + 2 < blocks))
        def _():
            for copy in fetch(i + 2):
                copy.start()

        rows = pl.ds(pl.multiple_of(i * block, block), block)
        products_ref[:, rows] = product(lhs[...], held[rows, :])
        total = to_lanes(squares(held, rows) + squares(others_ref, rows))
        scale_ref[:, rows] = lax.rsqrt(total + epsilon)
        return carry

    lax.fori_loop(0, blocks, step, 0)


def block_of(count, tiles):
    total = count // LANES
    while total % tiles:
        tiles -= 1
    return tiles * LANES


def near_products(me, pieces, classes):
    count, features = classes.shape
    chunks, (depth, rows) = len(pieces), pieces[0].shape
    width, block = features // 2, block_of(count, 8)
    blocks = count // block
    keep = pltpu.with_memory_space_constraint
    scalar, plain = [pl.BlockSpec(memory_space=pltpu.SMEM)], [pl.BlockSpec(memory_space=pltpu.HBM)]
    classes = keep(classes, pltpu.HBM)
    halves = VMEM((count, width), jnp.bfloat16)
    own, held, others = pl.pallas_call(
        functools.partial(load_body, chunks, block),
        out_shape=(VMEM((depth, rows), jnp.bfloat16), halves, halves),
        in_specs=scalar + plain * 2,
        out_specs=tuple(whole(3)),
        scratch_shapes=[pltpu.SemaphoreType.DMA(()), pltpu.SemaphoreType.DMA((2, 1))],
        cost_estimate=pl.CostEstimate(flops=0, bytes_accessed=2 * block * features, transcendentals=0),
        compiler_params=SMALL,
        name="load_first",
    )(me, keep(pieces[0], pltpu.HBM), classes)
    products, _, others, scale, square = pl.pallas_call(
        functools.partial(near_body, chunks, block),
        out_shape=(
            VMEM((rows, count), jnp.float32),
            halves,
            halves,
            VMEM((1, count), jnp.float32),
            VMEM((rows, LANES), jnp.float32),
        ),
        in_specs=scalar + whole(chunks) + plain + whole(2),
        out_specs=tuple(whole(5)),
        scratch_shapes=[
            VMEM((width, rows), jnp.bfloat16),
            VMEM((rows, width), jnp.bfloat16),
            pltpu.SemaphoreType.DMA((2, blocks)),
        ],
        input_output_aliases={2 + chunks: 1, 3 + chunks: 2},
        cost_estimate=pl.CostEstimate(
            flops=2 * rows * count * width, bytes_accessed=2 * count * features, transcendentals=0
        ),
        compiler_params=pltpu.CompilerParams(vmem_limit_bytes=8 << 20),
        name="near_products",
    )(me, keep(own, VMEM), *(keep(p, VMEM) for p in pieces[1:]), classes, keep(held, VMEM), keep(others, VMEM))
    return products, others, scale, square


def early_width(pieces, depth):
    return depth // 256 * 256 if pieces == 2 else 0


def early_body(early, me_ref, piece, products_ref, others_ref, square_ref, sums_ref, total_ref, lhs):
    depth, width = piece.shape[0], others_ref.shape[1]
    index = lax.rem(me_ref[0], 2)
    lhs[...] = piece[pl.ds(pl.multiple_of(index * (depth - early), 16), early), :].T
    total_ref[...] = square_ref[...] + squares(lhs)
    lanes = pl.ds(pl.multiple_of(index * (width - early), LANES), early)
    sums_ref[...] = products_ref[...] + product(lhs[...], others_ref[:, lanes])


def early_products(early, me, piece, products, others, square):
    rows, count = products.shape
    keep = pltpu.with_memory_space_constraint
    return pl.pallas_call(
        functools.partial(early_body, early),
        out_shape=(VMEM((rows, count), jnp.float32), VMEM((rows, LANES), jnp.float32)),
        in_specs=[pl.BlockSpec(memory_space=pltpu.SMEM)] + whole(4),
        out_specs=tuple(whole(2)),
        scratch_shapes=[VMEM((rows, early), jnp.bfloat16)],
        input_output_aliases={2: 0},
        cost_estimate=pl.CostEstimate(
            flops=2 * rows * count * early, bytes_accessed=8 * rows * count, transcendentals=0
        ),
        compiler_params=pltpu.CompilerParams(vmem_limit_bytes=16 << 20),
        name="early_products",
    )(me, keep(piece, VMEM), keep(products, VMEM), keep(others, VMEM), keep(square, VMEM))


def far_body(chunks, block, early, me_ref, *refs):
    pieces = refs[:chunks]
    products_ref, others_ref, scale_ref, square_ref, kernel_ref, sums_ref, turned, lhs, factor, part = refs[chunks:]
    place(pieces, turned, me_ref[0])
    start = pl.multiple_of(early - lax.rem(me_ref[0], 2) * early, LANES)
    lhs[...] = turned[pl.ds(start, lhs.shape[1]), :].T
    square = jnp.sum(square_ref[...] + squares(lhs), axis=1, keepdims=True)
    factor[...] = jnp.broadcast_to(logit_scale * lax.rsqrt(square + epsilon), factor.shape)
    part[...] = jnp.zeros_like(part)

    group = 64

    def step(i, carry):
        span = pl.ds(pl.multiple_of(i * block, block), block)
        view, scale = kernel_ref.at[:, span], scale_ref.at[:, span]
        view[...] = products_ref[:, span] + product(lhs[...], others_ref[span, pl.ds(start, lhs.shape[1])])
        for r in range(0, part.shape[0], group):
            rows = slice(r, r + group)
            total = part[rows, :]
            for at in range(0, block, LANES):
                lanes = slice(at, at + LANES)
                value = jnp.exp(view[rows, lanes] * factor[rows, :] * scale[:, lanes])
                view[rows, lanes] = value
                total = total + value
            part[rows, :] = total
        return carry

    lax.fori_loop(0, others_ref.shape[0] // block, step, 0)
    sums_ref[...] = to_lanes(part[...])


def far_kernel(early, me, pieces, products, others, scale, square):
    rows, count = products.shape
    width = others.shape[1]
    keep = pltpu.with_memory_space_constraint
    return pl.pallas_call(
        functools.partial(far_body, len(pieces), block_of(count, 20), early),
        out_shape=(VMEM((rows, count), jnp.float32), VMEM((1, rows), jnp.float32)),
        in_specs=[pl.BlockSpec(memory_space=pltpu.SMEM)] + whole(len(pieces) + 4),
        out_specs=tuple(whole(2)),
        scratch_shapes=[
            VMEM((width, rows), jnp.bfloat16),
            VMEM((rows, width - early), jnp.bfloat16),
            VMEM((rows, LANES), jnp.float32),
            VMEM((rows, LANES), jnp.float32),
        ],
        input_output_aliases={1 + len(pieces): 0},
        compiler_params=pltpu.CompilerParams(vmem_limit_bytes=16 << 20),
        name="far_kernel",
    )(me, *(keep(p, VMEM) for p in pieces), keep(products, VMEM), keep(others, VMEM), keep(scale, VMEM), keep(square, VMEM))


def added(refs):
    total = refs[0][...]
    for ref in refs[1:]:
        total = total + ref[...]
    return total


def column_body(kernel_ref, *refs):
    *sums, out_ref, spread, part = refs
    spread[...] = to_rows(1.0 / added(sums))
    rows, count = kernel_ref.shape
    group = 64
    part[...] = jnp.zeros_like(part)

    def chunk(i, carry):
        at = pl.ds(pl.multiple_of(i * group, group), group)
        view, scale = kernel_ref.at[at, :], spread[at, :]
        for j in range(0, count, LANES):
            lanes = slice(j, j + LANES)
            value = (view[:, lanes] * scale).reshape(group // 8, 8, LANES)
            part[:, lanes] += jnp.sum(value, axis=0)
        return carry

    lax.fori_loop(0, rows // group, chunk, 0)
    total = jnp.sum(part[...], axis=0, keepdims=True)
    out_ref[...] = jnp.broadcast_to(total[None], out_ref.shape)


def column_sums(kernel, sums, copies):
    rows, count = kernel.shape
    return pl.pallas_call(
        column_body,
        out_shape=VMEM((copies, 1, count), jnp.float32),
        in_specs=whole(1 + len(sums)),
        out_specs=whole(1)[0],
        scratch_shapes=[VMEM((rows, LANES), jnp.float32), VMEM((8, count), jnp.float32)],
        compiler_params=SMALL,
        name="column_sums",
    )(pltpu.with_memory_space_constraint(kernel, VMEM), *sums)


def row_body(kernel_ref, sums_ref, counts_ref, out_ref, scale_ref, part):
    scale_ref[...] = counts_ref[...].astype(jnp.float32) / jnp.sum(sums_ref[...], axis=0)
    rows, count = kernel_ref.shape
    group, block = 64, block_of(count, 8)
    part[...] = jnp.zeros_like(part)

    def chunk(j, carry):
        span = pl.ds(pl.multiple_of(j * block, block), block)
        view, scale = kernel_ref.at[:, span], scale_ref.at[:, span]
        for r in range(0, rows, group):
            at = slice(r, r + group)
            total = part[at, :]
            for k in range(0, block, LANES):
                total = total + view[at, k : k + LANES] * scale[:, k : k + LANES]
            part[at, :] = total
        return carry

    lax.fori_loop(0, count // block, chunk, 0)
    out_ref[...] = to_lanes(part[...])


def row_sums(kernel, sums, counts, last):
    rows, count = kernel.shape
    outputs = (VMEM((1, rows), jnp.float32), VMEM((1, count), jnp.float32))
    result = pl.pallas_call(
        row_body,
        out_shape=outputs[: 1 + last],
        in_specs=whole(3),
        out_specs=tuple(whole(1 + last)),
        scratch_shapes=[*outputs[1 + last :], VMEM((rows, LANES), jnp.float32)],
        compiler_params=SMALL,
        name="row_sums",
    )(pltpu.with_memory_space_constraint(kernel, VMEM), sums, counts)
    return result if last else (*result, None)


def assign_body(kernel_ref, scale_ref, *refs):
    *sums, out_ref, spread, ready, sems = refs
    spread[...] = to_rows(1.0 / added(sums))
    stripes, group, count = ready.shape

    def put(i):
        return pltpu.make_async_copy(ready.at[i], out_ref.at[pl.ds(i * group, group), :], sems.at[i])

    def step(i, carry):
        at = pl.ds(pl.multiple_of(i * group, group), group)
        for j in range(count // LANES):
            lanes = slice(j * LANES, (j + 1) * LANES)
            value = spread[at, :] * kernel_ref[at, lanes] * scale_ref[:, lanes]
            ready[i, :, lanes] = value.astype(jnp.bfloat16)
        put(i).start()
        return carry

    lax.fori_loop(0, stripes, step, 0)
    for i in range(stripes):
        put(i).wait()


def assign(kernel, scale, sums):
    rows, count = kernel.shape
    group = 64
    return pl.pallas_call(
        assign_body,
        out_shape=jax.ShapeDtypeStruct((rows, count), jnp.bfloat16),
        in_specs=whole(2 + len(sums)),
        out_specs=pl.BlockSpec(memory_space=pl.ANY),
        scratch_shapes=[
            VMEM((rows, LANES), jnp.float32),
            VMEM((rows // group, group, count), jnp.bfloat16),
            pltpu.SemaphoreType.DMA((rows // group,)),
        ],
        compiler_params=SMALL,
        name="assign",
    )(pltpu.with_memory_space_constraint(kernel, VMEM), scale, *sums)


def gathered(piece, steps):
    held = [piece]
    for bit in steps:
        held = held + [exchange(h, "cls", bit) for h in held]
    return held


def shards(shapes, classes, counts):
    *low, top = bits("cls")
    me = jnp.reshape(lax.axis_index("cls"), (1,)).astype(jnp.int32)
    mine = shapes.T
    other = exchange(mine, "cls", top)
    products, others, scale, square = near_products(me, gathered(mine, low), classes)
    square, other = lax.optimization_barrier((square, other))
    pieces = gathered(other, low)
    early = early_width(len(pieces), mine.shape[0])
    if early:
        products, square = early_products(early, me, other, products, others, square)
    kernel, sums = far_kernel(early, me, pieces, products, others, scale, square)
    target = counts[None, :]
    for step in range(ITERS):
        copies = column_sums(kernel, terms(sums, "cls"), lax.axis_size("shape"))
        columns = lax.all_to_all(copies, "shape", 0, 0)
        sums, col_scale = row_sums(kernel, columns, target, step == ITERS - 1)
    return assign(kernel, col_scale, terms(sums, "cls"))


def solution(mesh):
    placed = (P("shape", "cls"), P("cls", None), P("cls"))
    return jax.shard_map(
        shards, mesh=mesh, in_specs=placed, out_specs=P("shape", "cls"), check_vma=False
    )
```

```python
import functools

import jax
import jax.numpy as jnp
from jax import lax
from jax.experimental import pallas as pl
from jax.experimental.pallas import tpu as pltpu
from jax.sharding import PartitionSpec as P

ITERS = 3

logit_scale = 40.0
epsilon = 1e-06
LANES = 128
VMEM = pltpu.VMEM
SMALL = pltpu.CompilerParams(vmem_limit_bytes=16 << 20)


def bits(axis):
    size = lax.axis_size(axis)
    assert size & (size - 1) == 0
    return [1 << b for b in range(size.bit_length() - 1)]


def exchange(value, axis, bit):
    size = lax.axis_size(axis)
    return lax.ppermute(value, axis, [(i, i ^ bit) for i in range(size)])


def terms(value, axis):
    parts, steps = [value], bits(axis)
    for at in range(0, len(steps), 2):
        value = sum(parts[1:], parts[0])
        offsets = [0]
        for bit in steps[at : at + 2]:
            offsets = offsets + [o ^ bit for o in offsets]
        parts = [value] + [exchange(value, axis, o) for o in offsets[1:]]
    return parts


def whole(count):
    return [pl.BlockSpec(memory_space=VMEM)] * count


def tile(index):
    return pl.ds(pl.multiple_of(index * LANES, LANES), LANES)


def to_lanes(value):
    return jnp.sum(value.T, axis=0, keepdims=True)


def to_rows(value):
    return jnp.broadcast_to(value, (LANES, value.shape[1])).T


def slot(pieces, turned, me, offset):
    depth = turned.shape[0] // pieces
    index = lax.bitwise_and(lax.bitwise_xor(me, offset), pieces - 1)
    return turned.at[pl.ds(pl.multiple_of(index * depth, depth), depth), :]


def place(pieces, turned, me, start=0):
    for offset in range(start, len(pieces)):
        slot(len(pieces), turned, me, offset)[...] = pieces[offset][...]


def squares(value_ref, at=slice(None)):
    total = None
    for t in range(value_ref.shape[1] // LANES):
        value = value_ref[at, t * LANES : (t + 1) * LANES].astype(jnp.float32)
        total = value * value if total is None else total + value * value
    return total


def product(lhs, rhs):
    return lax.dot_general(lhs, rhs, (((1,), (1,)), ((), ())), preferred_element_type=jnp.float32)


def near_body(chunks, block, ahead, me_ref, *refs):
    pieces = refs[:chunks]
    classes_ref, products_ref, others_ref, scale_ref, square_ref, turned, lhs, own, held, sems = refs[chunks:]
    width, blocks = lhs.shape[1], held.shape[0]
    me = me_ref[0]
    mine = lax.div(me, chunks)

    def fetch(i):
        rows = pl.ds(pl.multiple_of(i * block, block), block)
        near = pl.ds(pl.multiple_of(mine * width, LANES), width)
        far = pl.ds(pl.multiple_of((1 - mine) * width, LANES), width)
        return (
            pltpu.make_async_copy(classes_ref.at[rows, near], held.at[i], sems.at[0, i]),
            pltpu.make_async_copy(classes_ref.at[rows, far], others_ref.at[rows, :], sems.at[1, i]),
        )

    first = pltpu.make_async_copy(pieces[0], slot(chunks, turned, me, 0), own)
    first.start()
    for i in range(min(ahead, blocks)):
        for copy in fetch(i):
            copy.start()
    place(pieces, turned, me, 1)
    first.wait()
    lhs[...] = turned[...].T
    square_ref[...] = squares(lhs)

    def step(i, carry):
        @pl.when(i + ahead < blocks)
        def _():
            for copy in fetch(i + ahead):
                copy.start()

        for copy in fetch(i):
            copy.wait()
        rows = pl.ds(pl.multiple_of(i * block, block), block)
        products_ref[:, rows] = product(lhs[...], held[i])
        total = to_lanes(squares(held.at[i]) + squares(others_ref, rows))
        scale_ref[:, rows] = lax.rsqrt(total + epsilon)
        return carry

    lax.fori_loop(0, blocks, step, 0)


def block_of(count, tiles):
    total = count // LANES
    while total % tiles:
        tiles -= 1
    return tiles * LANES


def near_products(me, pieces, classes):
    count, features = classes.shape
    chunks, rows = len(pieces), pieces[0].shape[1]
    width, block = features // 2, block_of(count, 8)
    blocks = count // block
    keep = pltpu.with_memory_space_constraint
    plain = [pl.BlockSpec(memory_space=pltpu.HBM)]
    return pl.pallas_call(
        functools.partial(near_body, chunks, block, 2),
        out_shape=(
            VMEM((rows, count), jnp.float32),
            VMEM((count, width), jnp.bfloat16),
            VMEM((1, count), jnp.float32),
            VMEM((rows, LANES), jnp.float32),
        ),
        in_specs=[pl.BlockSpec(memory_space=pltpu.SMEM)] + plain + whole(chunks - 1) + plain,
        out_specs=tuple(whole(4)),
        scratch_shapes=[
            VMEM((width, rows), jnp.bfloat16),
            VMEM((rows, width), jnp.bfloat16),
            pltpu.SemaphoreType.DMA(()),
            VMEM((blocks, block, width), jnp.bfloat16),
            pltpu.SemaphoreType.DMA((2, blocks)),
        ],
        cost_estimate=pl.CostEstimate(
            flops=2 * rows * count * width, bytes_accessed=2 * count * features, transcendentals=0
        ),
        compiler_params=pltpu.CompilerParams(vmem_limit_bytes=32 << 20),
        name="near_products",
    )(me, keep(pieces[0], pltpu.HBM), *(keep(p, VMEM) for p in pieces[1:]), keep(classes, pltpu.HBM))


def early_width(pieces, depth):
    return depth // 256 * 256 if pieces == 2 else 0


def early_body(early, me_ref, piece, products_ref, others_ref, square_ref, sums_ref, total_ref, lhs):
    depth, width = piece.shape[0], others_ref.shape[1]
    index = lax.rem(me_ref[0], 2)
    lhs[...] = piece[pl.ds(pl.multiple_of(index * (depth - early), 16), early), :].T
    total_ref[...] = square_ref[...] + squares(lhs)
    lanes = pl.ds(pl.multiple_of(index * (width - early), LANES), early)
    sums_ref[...] = products_ref[...] + product(lhs[...], others_ref[:, lanes])


def early_products(early, me, piece, products, others, square):
    rows, count = products.shape
    keep = pltpu.with_memory_space_constraint
    return pl.pallas_call(
        functools.partial(early_body, early),
        out_shape=(VMEM((rows, count), jnp.float32), VMEM((rows, LANES), jnp.float32)),
        in_specs=[pl.BlockSpec(memory_space=pltpu.SMEM)] + whole(4),
        out_specs=tuple(whole(2)),
        scratch_shapes=[VMEM((rows, early), jnp.bfloat16)],
        input_output_aliases={2: 0},
        cost_estimate=pl.CostEstimate(
            flops=2 * rows * count * early, bytes_accessed=8 * rows * count, transcendentals=0
        ),
        compiler_params=pltpu.CompilerParams(vmem_limit_bytes=24 << 20),
        name="early_products",
    )(me, keep(piece, VMEM), keep(products, VMEM), keep(others, VMEM), keep(square, VMEM))


def far_body(chunks, block, early, me_ref, *refs):
    pieces = refs[:chunks]
    products_ref, others_ref, scale_ref, square_ref, kernel_ref, sums_ref, turned, lhs, factor, part = refs[chunks:]
    place(pieces, turned, me_ref[0])
    start = pl.multiple_of(early - lax.rem(me_ref[0], 2) * early, LANES)
    lhs[...] = turned[pl.ds(start, lhs.shape[1]), :].T
    square = jnp.sum(square_ref[...] + squares(lhs), axis=1, keepdims=True)
    factor[...] = jnp.broadcast_to(logit_scale * lax.rsqrt(square + epsilon), factor.shape)
    part[...] = jnp.zeros_like(part)

    group = 64

    def step(i, carry):
        span = pl.ds(pl.multiple_of(i * block, block), block)
        view, scale = kernel_ref.at[:, span], scale_ref.at[:, span]
        view[...] = products_ref[:, span] + product(lhs[...], others_ref[span, pl.ds(start, lhs.shape[1])])
        for r in range(0, part.shape[0], group):
            rows = slice(r, r + group)
            total = part[rows, :]
            for at in range(0, block, LANES):
                lanes = slice(at, at + LANES)
                value = jnp.exp(view[rows, lanes] * factor[rows, :] * scale[:, lanes])
                view[rows, lanes] = value
                total = total + value
            part[rows, :] = total
        return carry

    lax.fori_loop(0, others_ref.shape[0] // block, step, 0)
    sums_ref[...] = to_lanes(part[...])


def far_kernel(early, me, pieces, products, others, scale, square):
    rows, count = products.shape
    width = others.shape[1]
    keep = pltpu.with_memory_space_constraint
    return pl.pallas_call(
        functools.partial(far_body, len(pieces), block_of(count, 20), early),
        out_shape=(VMEM((rows, count), jnp.float32), VMEM((1, rows), jnp.float32)),
        in_specs=[pl.BlockSpec(memory_space=pltpu.SMEM)] + whole(len(pieces) + 4),
        out_specs=tuple(whole(2)),
        scratch_shapes=[
            VMEM((width, rows), jnp.bfloat16),
            VMEM((rows, width - early), jnp.bfloat16),
            VMEM((rows, LANES), jnp.float32),
            VMEM((rows, LANES), jnp.float32),
        ],
        input_output_aliases={1 + len(pieces): 0},
        compiler_params=pltpu.CompilerParams(vmem_limit_bytes=32 << 20),
        name="far_kernel",
    )(me, *(keep(p, VMEM) for p in pieces), keep(products, VMEM), keep(others, VMEM), keep(scale, VMEM), keep(square, VMEM))


def added(refs):
    total = refs[0][...]
    for ref in refs[1:]:
        total = total + ref[...]
    return total


def column_body(kernel_ref, *refs):
    *sums, out_ref, spread, part, total = refs
    spread[...] = to_rows(1.0 / added(sums))
    rows, count = kernel_ref.shape
    group = 64
    part[...] = jnp.zeros_like(part)

    def chunk(i, carry):
        at = pl.ds(pl.multiple_of(i * group, group), group)
        view, scale = kernel_ref.at[at, :], spread[at, :]
        for j in range(0, count, LANES):
            lanes = slice(j, j + LANES)
            value = (view[:, lanes] * scale).reshape(group // 8, 8, LANES)
            part[:, lanes] += jnp.sum(value, axis=0)
        return carry

    lax.fori_loop(0, rows // group, chunk, 0)
    for j in range(count // LANES):
        total[j : j + 1, :] = jnp.sum(part[:, j * LANES : (j + 1) * LANES], axis=0, keepdims=True)
    out_ref[...] = jnp.broadcast_to(total[...][None], out_ref.shape)


def column_sums(kernel, sums, copies):
    rows, count = kernel.shape
    return pl.pallas_call(
        column_body,
        out_shape=VMEM((copies, count // LANES, LANES), jnp.float32),
        in_specs=whole(1 + len(sums)),
        out_specs=whole(1)[0],
        scratch_shapes=[
            VMEM((rows, LANES), jnp.float32),
            VMEM((8, count), jnp.float32),
            VMEM((count // LANES, LANES), jnp.float32),
        ],
        compiler_params=SMALL,
        name="column_sums",
    )(pltpu.with_memory_space_constraint(kernel, VMEM), *sums)


def row_body(kernel_ref, sums_ref, counts_ref, out_ref, scale_ref, part):
    scale_ref[...] = counts_ref[...].astype(jnp.float32) / jnp.sum(sums_ref[...], axis=0)
    rows, count = kernel_ref.shape
    group, block = 64, block_of(count, 8)
    part[...] = jnp.zeros_like(part)

    def chunk(j, carry):
        span = pl.ds(pl.multiple_of(j * block, block), block)
        view, scale = kernel_ref.at[:, span], scale_ref.at[pl.ds(j * (block // LANES), block // LANES), :]
        for r in range(0, rows, group):
            at = slice(r, r + group)
            total = part[at, :]
            for k in range(block // LANES):
                total = total + view[at, k * LANES : (k + 1) * LANES] * scale[k : k + 1, :]
            part[at, :] = total
        return carry

    lax.fori_loop(0, count // block, chunk, 0)
    out_ref[...] = to_lanes(part[...])


def row_sums(kernel, sums, counts, last):
    rows, count = kernel.shape
    outputs = (VMEM((1, rows), jnp.float32), VMEM(counts.shape, jnp.float32))
    result = pl.pallas_call(
        row_body,
        out_shape=outputs[: 1 + last],
        in_specs=whole(3),
        out_specs=tuple(whole(1 + last)),
        scratch_shapes=[*outputs[1 + last :], VMEM((rows, LANES), jnp.float32)],
        compiler_params=SMALL,
        name="row_sums",
    )(pltpu.with_memory_space_constraint(kernel, VMEM), sums, counts)
    return result if last else (*result, None)


def assign_body(kernel_ref, scale_ref, *refs):
    *sums, out_ref, spread, ready, sems = refs
    spread[...] = to_rows(1.0 / added(sums))
    stripes, group, count = ready.shape

    def put(i):
        return pltpu.make_async_copy(ready.at[i], out_ref.at[pl.ds(i * group, group), :], sems.at[i])

    def step(i, carry):
        at = pl.ds(pl.multiple_of(i * group, group), group)
        for j in range(count // LANES):
            lanes = slice(j * LANES, (j + 1) * LANES)
            value = spread[at, :] * kernel_ref[at, lanes] * scale_ref[j : j + 1, :]
            ready[i, :, lanes] = value.astype(jnp.bfloat16)
        put(i).start()
        return carry

    lax.fori_loop(0, stripes, step, 0)
    for i in range(stripes):
        put(i).wait()


def assign(kernel, scale, sums):
    rows, count = kernel.shape
    group = 64
    return pl.pallas_call(
        assign_body,
        out_shape=jax.ShapeDtypeStruct((rows, count), jnp.bfloat16),
        in_specs=whole(2 + len(sums)),
        out_specs=pl.BlockSpec(memory_space=pl.ANY),
        scratch_shapes=[
            VMEM((rows, LANES), jnp.float32),
            VMEM((rows // group, group, count), jnp.bfloat16),
            pltpu.SemaphoreType.DMA((rows // group,)),
        ],
        compiler_params=SMALL,
        name="assign",
    )(pltpu.with_memory_space_constraint(kernel, VMEM), scale, *sums)


def gathered(piece, steps):
    held = [piece]
    for bit in steps:
        held = held + [exchange(h, "cls", bit) for h in held]
    return held


def shards(shapes, classes, counts):
    *low, top = bits("cls")
    me = jnp.reshape(lax.axis_index("cls"), (1,)).astype(jnp.int32)
    mine = shapes.T
    other = exchange(mine, "cls", top)
    products, others, scale, square = near_products(me, gathered(mine, low), classes)
    square, other = lax.optimization_barrier((square, other))
    pieces = gathered(other, low)
    early = early_width(len(pieces), mine.shape[0])
    if early:
        products, square = early_products(early, me, other, products, others, square)
    kernel, sums = far_kernel(early, me, pieces, products, others, scale, square)
    target = counts.reshape(-1, LANES)
    for step in range(ITERS):
        copies = column_sums(kernel, terms(sums, "cls"), lax.axis_size("shape"))
        columns = lax.all_to_all(copies, "shape", 0, 0)
        sums, col_scale = row_sums(kernel, columns, target, step == ITERS - 1)
    return assign(kernel, col_scale, terms(sums, "cls"))


def solution(mesh):
    placed = (P("shape", "cls"), P("cls", None), P("cls"))
    return jax.shard_map(
        shards, mesh=mesh, in_specs=placed, out_specs=P("shape", "cls"), check_vma=False
    )
```

```python
import functools

import jax
import jax.numpy as jnp
from jax import lax
from jax.experimental import pallas as pl
from jax.experimental.pallas import tpu as pltpu
from jax.sharding import PartitionSpec as P

ITERS = 3

logit_scale = 40.0
epsilon = 1e-06
LANES = 128
VMEM = pltpu.VMEM
SMALL = pltpu.CompilerParams(vmem_limit_bytes=16 << 20)


def bits(axis):
    size = lax.axis_size(axis)
    assert size & (size - 1) == 0
    return [1 << b for b in range(size.bit_length() - 1)]


def exchange(value, axis, bit):
    size = lax.axis_size(axis)
    return lax.ppermute(value, axis, [(i, i ^ bit) for i in range(size)])


def terms(value, axis):
    parts, steps = [value], bits(axis)
    for at in range(0, len(steps), 2):
        value = sum(parts[1:], parts[0])
        offsets = [0]
        for bit in steps[at : at + 2]:
            offsets = offsets + [o ^ bit for o in offsets]
        parts = [value] + [exchange(value, axis, o) for o in offsets[1:]]
    return parts


def whole(count):
    return [pl.BlockSpec(memory_space=VMEM)] * count


def to_lanes(value):
    return jnp.sum(value.T, axis=0, keepdims=True)


def to_rows(value):
    return jnp.broadcast_to(value, (LANES, value.shape[1])).T


def slot(pieces, turned, me, offset):
    depth = turned.shape[0] // pieces
    index = lax.bitwise_and(lax.bitwise_xor(me, offset), pieces - 1)
    return turned.at[pl.ds(pl.multiple_of(index * depth, depth), depth), :]


def place(pieces, turned, me, start=0):
    for offset in range(start, len(pieces)):
        slot(len(pieces), turned, me, offset)[...] = pieces[offset][...]


def squares(value_ref, at=slice(None)):
    total = None
    for t in range(value_ref.shape[1] // LANES):
        value = value_ref[at, t * LANES : (t + 1) * LANES].astype(jnp.float32)
        total = value * value if total is None else total + value * value
    return total


def product(lhs, rhs):
    return lax.dot_general(lhs, rhs, (((1,), (1,)), ((), ())), preferred_element_type=jnp.float32)


def near_body(chunks, block, ahead, me_ref, *refs):
    pieces = refs[:chunks]
    classes_ref, products_ref, others_ref, scale_ref, square_ref, turned, lhs, own, held, sems = refs[chunks:]
    width, blocks = lhs.shape[1], held.shape[0]
    me = me_ref[0]
    mine = lax.div(me, chunks)

    def fetch(i):
        rows = pl.ds(pl.multiple_of(i * block, block), block)
        near = pl.ds(pl.multiple_of(mine * width, LANES), width)
        far = pl.ds(pl.multiple_of((1 - mine) * width, LANES), width)
        return (
            pltpu.make_async_copy(classes_ref.at[rows, near], held.at[i], sems.at[0, i]),
            pltpu.make_async_copy(classes_ref.at[rows, far], others_ref.at[rows, :], sems.at[1, i]),
        )

    first = pltpu.make_async_copy(pieces[0], slot(chunks, turned, me, 0), own)
    first.start()
    for i in range(min(ahead, blocks)):
        for copy in fetch(i):
            copy.start()
    place(pieces, turned, me, 1)
    first.wait()
    lhs[...] = turned[...].T
    square_ref[...] = squares(lhs)

    def step(i, carry):
        @pl.when(i + ahead < blocks)
        def _():
            for copy in fetch(i + ahead):
                copy.start()

        for copy in fetch(i):
            copy.wait()
        rows = pl.ds(pl.multiple_of(i * block, block), block)
        products_ref[:, rows] = product(lhs[...], held[i])
        total = to_lanes(squares(held.at[i]) + squares(others_ref, rows))
        scale_ref[:, rows] = lax.rsqrt(total + epsilon)
        return carry

    lax.fori_loop(0, blocks, step, 0)


def block_of(count, tiles):
    total = count // LANES
    while total % tiles:
        tiles -= 1
    return tiles * LANES


def near_products(me, pieces, classes):
    count, features = classes.shape
    chunks, rows = len(pieces), pieces[0].shape[1]
    width, block = features // 2, block_of(count, 8)
    blocks = count // block
    keep = pltpu.with_memory_space_constraint
    plain = [pl.BlockSpec(memory_space=pltpu.HBM)]
    return pl.pallas_call(
        functools.partial(near_body, chunks, block, 2),
        out_shape=(
            VMEM((rows, count), jnp.float32),
            VMEM((count, width), jnp.bfloat16),
            VMEM((1, count), jnp.float32),
            VMEM((rows, LANES), jnp.float32),
        ),
        in_specs=[pl.BlockSpec(memory_space=pltpu.SMEM)] + plain + whole(chunks - 1) + plain,
        out_specs=tuple(whole(4)),
        scratch_shapes=[
            VMEM((width, rows), jnp.bfloat16),
            VMEM((rows, width), jnp.bfloat16),
            pltpu.SemaphoreType.DMA(()),
            VMEM((blocks, block, width), jnp.bfloat16),
            pltpu.SemaphoreType.DMA((2, blocks)),
        ],
        cost_estimate=pl.CostEstimate(
            flops=2 * rows * count * width, bytes_accessed=2 * count * features, transcendentals=0
        ),
        compiler_params=pltpu.CompilerParams(vmem_limit_bytes=32 << 20),
        name="near_products",
    )(me, keep(pieces[0], pltpu.HBM), *(keep(p, VMEM) for p in pieces[1:]), keep(classes, pltpu.HBM))


def early_width(pieces, depth):
    return depth // 256 * 256 if pieces == 2 else 0


def early_body(early, me_ref, piece, products_ref, others_ref, square_ref, sums_ref, total_ref, lhs):
    depth, width = piece.shape[0], others_ref.shape[1]
    index = lax.rem(me_ref[0], 2)
    lhs[...] = piece[pl.ds(pl.multiple_of(index * (depth - early), 16), early), :].T
    total_ref[...] = square_ref[...] + squares(lhs)
    lanes = pl.ds(pl.multiple_of(index * (width - early), LANES), early)
    sums_ref[...] = products_ref[...] + product(lhs[...], others_ref[:, lanes])


def early_products(early, me, piece, products, others, square):
    rows, count = products.shape
    keep = pltpu.with_memory_space_constraint
    return pl.pallas_call(
        functools.partial(early_body, early),
        out_shape=(VMEM((rows, count), jnp.float32), VMEM((rows, LANES), jnp.float32)),
        in_specs=[pl.BlockSpec(memory_space=pltpu.SMEM)] + whole(4),
        out_specs=tuple(whole(2)),
        scratch_shapes=[VMEM((rows, early), jnp.bfloat16)],
        input_output_aliases={2: 0},
        cost_estimate=pl.CostEstimate(
            flops=2 * rows * count * early, bytes_accessed=8 * rows * count, transcendentals=0
        ),
        compiler_params=pltpu.CompilerParams(vmem_limit_bytes=24 << 20),
        name="early_products",
    )(me, keep(piece, VMEM), keep(products, VMEM), keep(others, VMEM), keep(square, VMEM))


def far_body(chunks, block, early, me_ref, *refs):
    pieces = refs[:chunks]
    products_ref, others_ref, scale_ref, square_ref, kernel_ref, sums_ref, turned, lhs, factor, part = refs[chunks:]
    place(pieces, turned, me_ref[0])
    start = pl.multiple_of(early - lax.rem(me_ref[0], 2) * early, LANES)
    lhs[...] = turned[pl.ds(start, lhs.shape[1]), :].T
    square = jnp.sum(square_ref[...] + squares(lhs), axis=1, keepdims=True)
    factor[...] = jnp.broadcast_to(logit_scale * lax.rsqrt(square + epsilon), factor.shape)
    part[...] = jnp.zeros_like(part)

    group = 64

    def step(i, carry):
        span = pl.ds(pl.multiple_of(i * block, block), block)
        view, scale = kernel_ref.at[:, span], scale_ref.at[:, span]
        view[...] = products_ref[:, span] + product(lhs[...], others_ref[span, pl.ds(start, lhs.shape[1])])
        for r in range(0, part.shape[0], group):
            rows = slice(r, r + group)
            total = part[rows, :]
            for at in range(0, block, LANES):
                lanes = slice(at, at + LANES)
                value = jnp.exp(view[rows, lanes] * factor[rows, :] * scale[:, lanes])
                view[rows, lanes] = value
                total = total + value
            part[rows, :] = total
        return carry

    lax.fori_loop(0, others_ref.shape[0] // block, step, 0)
    sums_ref[...] = to_lanes(part[...])


def far_kernel(early, me, pieces, products, others, scale, square):
    rows, count = products.shape
    width = others.shape[1]
    keep = pltpu.with_memory_space_constraint
    return pl.pallas_call(
        functools.partial(far_body, len(pieces), block_of(count, 20), early),
        out_shape=(VMEM((rows, count), jnp.float32), VMEM((1, rows), jnp.float32)),
        in_specs=[pl.BlockSpec(memory_space=pltpu.SMEM)] + whole(len(pieces) + 4),
        out_specs=tuple(whole(2)),
        scratch_shapes=[
            VMEM((width, rows), jnp.bfloat16),
            VMEM((rows, width - early), jnp.bfloat16),
            VMEM((rows, LANES), jnp.float32),
            VMEM((rows, LANES), jnp.float32),
        ],
        input_output_aliases={1 + len(pieces): 0},
        compiler_params=pltpu.CompilerParams(vmem_limit_bytes=32 << 20),
        name="far_kernel",
    )(me, *(keep(p, VMEM) for p in pieces), keep(products, VMEM), keep(others, VMEM), keep(scale, VMEM), keep(square, VMEM))


def added(refs):
    total = refs[0][...]
    for ref in refs[1:]:
        total = total + ref[...]
    return total


def column_body(kernel_ref, *refs):
    *sums, out_ref, spread, part, total = refs
    spread[...] = to_rows(1.0 / added(sums))
    rows, count = kernel_ref.shape
    group = 64
    part[...] = jnp.zeros_like(part)

    def chunk(i, carry):
        at = pl.ds(pl.multiple_of(i * group, group), group)
        view, scale = kernel_ref.at[at, :], spread[at, :]
        for j in range(0, count, LANES):
            lanes = slice(j, j + LANES)
            value = (view[:, lanes] * scale).reshape(group // 8, 8, LANES)
            part[:, lanes] += jnp.sum(value, axis=0)
        return carry

    lax.fori_loop(0, rows // group, chunk, 0)
    for j in range(count // LANES):
        total[j : j + 1, :] = jnp.sum(part[:, j * LANES : (j + 1) * LANES], axis=0, keepdims=True)
    out_ref[...] = jnp.broadcast_to(total[...][None], out_ref.shape)


def column_sums(kernel, sums, copies):
    rows, count = kernel.shape
    return pl.pallas_call(
        column_body,
        out_shape=VMEM((copies, count // LANES, LANES), jnp.float32),
        in_specs=whole(1 + len(sums)),
        out_specs=whole(1)[0],
        scratch_shapes=[
            VMEM((rows, LANES), jnp.float32),
            VMEM((8, count), jnp.float32),
            VMEM((count // LANES, LANES), jnp.float32),
        ],
        compiler_params=SMALL,
        name="column_sums",
    )(pltpu.with_memory_space_constraint(kernel, VMEM), *sums)


def row_body(kernel_ref, sums_ref, counts_ref, out_ref, scale_ref, part):
    scale_ref[...] = counts_ref[...].astype(jnp.float32) / jnp.sum(sums_ref[...], axis=0)
    rows, count = kernel_ref.shape
    group, block = 64, block_of(count, 8)
    part[...] = jnp.zeros_like(part)

    def chunk(j, carry):
        span = pl.ds(pl.multiple_of(j * block, block), block)
        view, scale = kernel_ref.at[:, span], scale_ref.at[pl.ds(j * (block // LANES), block // LANES), :]
        for r in range(0, rows, group):
            at = slice(r, r + group)
            total = part[at, :]
            for k in range(block // LANES):
                total = total + view[at, k * LANES : (k + 1) * LANES] * scale[k : k + 1, :]
            part[at, :] = total
        return carry

    lax.fori_loop(0, count // block, chunk, 0)
    out_ref[...] = to_lanes(part[...])


def row_sums(kernel, sums, counts, last):
    rows, _ = kernel.shape
    outputs = (VMEM((1, rows), jnp.float32), VMEM(counts.shape, jnp.float32))
    result = pl.pallas_call(
        row_body,
        out_shape=outputs[: 1 + last],
        in_specs=whole(3),
        out_specs=tuple(whole(1 + last)),
        scratch_shapes=[*outputs[1 + last :], VMEM((rows, LANES), jnp.float32)],
        compiler_params=SMALL,
        name="row_sums",
    )(pltpu.with_memory_space_constraint(kernel, VMEM), sums, counts)
    return result if last else (*result, None)


def assign_body(kernel_ref, scale_ref, *refs):
    *sums, out_ref, spread, ready, sems = refs
    spread[...] = to_rows(1.0 / added(sums))
    stripes, group, count = ready.shape

    def put(i):
        return pltpu.make_async_copy(ready.at[i], out_ref.at[pl.ds(i * group, group), :], sems.at[i])

    def step(i, carry):
        at = pl.ds(pl.multiple_of(i * group, group), group)
        for j in range(count // LANES):
            lanes = slice(j * LANES, (j + 1) * LANES)
            value = spread[at, :] * kernel_ref[at, lanes] * scale_ref[j : j + 1, :]
            ready[i, :, lanes] = value.astype(jnp.bfloat16)
        put(i).start()
        return carry

    lax.fori_loop(0, stripes, step, 0)
    for i in range(stripes):
        put(i).wait()


def assign(kernel, scale, sums):
    rows, count = kernel.shape
    group = 64
    return pl.pallas_call(
        assign_body,
        out_shape=jax.ShapeDtypeStruct((rows, count), jnp.bfloat16),
        in_specs=whole(2 + len(sums)),
        out_specs=pl.BlockSpec(memory_space=pl.ANY),
        scratch_shapes=[
            VMEM((rows, LANES), jnp.float32),
            VMEM((rows // group, group, count), jnp.bfloat16),
            pltpu.SemaphoreType.DMA((rows // group,)),
        ],
        compiler_params=SMALL,
        name="assign",
    )(pltpu.with_memory_space_constraint(kernel, VMEM), scale, *sums)


def gathered(piece, steps):
    held = [piece]
    for bit in steps:
        held = held + [exchange(h, "cls", bit) for h in held]
    return held


def shards(shapes, classes, counts):
    *low, top = bits("cls")
    me = jnp.reshape(lax.axis_index("cls"), (1,)).astype(jnp.int32)
    mine = shapes.T
    other = exchange(mine, "cls", top)
    mine_too = gathered(mine, low)
    products, others, scale, square = near_products(me, mine_too, classes)
    square, other = lax.optimization_barrier((square, other))
    pieces = gathered(other, low)
    early = early_width(len(pieces), mine.shape[0])
    if early:
        products, square = early_products(early, me, other, products, others, square)
    kernel, sums = far_kernel(early, me, pieces, products, others, scale, square)
    target = counts.reshape(-1, LANES)
    for step in range(ITERS):
        copies = column_sums(kernel, terms(sums, "cls"), lax.axis_size("shape"))
        columns = lax.all_to_all(copies, "shape", 0, 0)
        sums, col_scale = row_sums(kernel, columns, target, step == ITERS - 1)
    return assign(kernel, col_scale, terms(sums, "cls"))


def solution(mesh):
    placed = (P("shape", "cls"), P("cls", None), P("cls"))
    return jax.shard_map(
        shards, mesh=mesh, in_specs=placed, out_specs=P("shape", "cls"), check_vma=False
    )
```

```python
import functools

import jax
import jax.numpy as jnp
from jax import lax
from jax.experimental import pallas as pl
from jax.experimental.pallas import tpu as pltpu
from jax.sharding import PartitionSpec as P

ITERS = 3

logit_scale = 40.0
epsilon = 1e-06
LANES = 128
VMEM = pltpu.VMEM
SMALL = pltpu.CompilerParams(vmem_limit_bytes=16 << 20)


def bits(axis):
    size = lax.axis_size(axis)
    assert size & (size - 1) == 0
    return [1 << b for b in range(size.bit_length() - 1)]


def exchange(value, axis, bit):
    size = lax.axis_size(axis)
    return lax.ppermute(value, axis, [(i, i ^ bit) for i in range(size)])


def terms(value, axis):
    parts, steps = [value], bits(axis)
    for at in range(0, len(steps), 2):
        value = sum(parts[1:], parts[0])
        offsets = [0]
        for bit in steps[at : at + 2]:
            offsets = offsets + [o ^ bit for o in offsets]
        parts = [value] + [exchange(value, axis, o) for o in offsets[1:]]
    return parts


def whole(count):
    return [pl.BlockSpec(memory_space=VMEM)] * count


def to_lanes(value):
    return jnp.sum(value.T, axis=0, keepdims=True)


def to_rows(value):
    return jnp.broadcast_to(value, (LANES, value.shape[1])).T


def slot(pieces, turned, me, offset):
    depth = turned.shape[0] // pieces
    index = lax.bitwise_and(lax.bitwise_xor(me, offset), pieces - 1)
    return turned.at[pl.ds(pl.multiple_of(index * depth, depth), depth), :]


def place(pieces, turned, me):
    for offset in range(len(pieces)):
        slot(len(pieces), turned, me, offset)[...] = pieces[offset][...]


def squares(value_ref, at=slice(None)):
    total = None
    for t in range(value_ref.shape[1] // LANES):
        value = value_ref[at, t * LANES : (t + 1) * LANES].astype(jnp.float32)
        total = value * value if total is None else total + value * value
    return total


def product(lhs, rhs):
    return lax.dot_general(lhs, rhs, (((1,), (1,)), ((), ())), preferred_element_type=jnp.float32)


def fetcher(mine, block, width, classes_ref, held, others_ref, sems):
    def fetch(i):
        rows = pl.ds(pl.multiple_of(i * block, block), block)
        near = pl.ds(pl.multiple_of(mine * width, LANES), width)
        far = pl.ds(pl.multiple_of((1 - mine) * width, LANES), width)
        return (
            pltpu.make_async_copy(classes_ref.at[rows, near], held.at[rows, :], sems.at[0, i]),
            pltpu.make_async_copy(classes_ref.at[rows, far], others_ref.at[rows, :], sems.at[1, i]),
        )

    return fetch


def load_body(chunks, block, me_ref, piece, classes_ref, own_ref, held, others_ref, sem, sems):
    fetch = fetcher(lax.div(me_ref[0], chunks), block, held.shape[1], classes_ref, held, others_ref, sems)
    copies = (pltpu.make_async_copy(piece, own_ref, sem), *fetch(0))
    for copy in copies:
        copy.start()
    for copy in copies:
        copy.wait()


def near_body(chunks, block, me_ref, *refs):
    pieces = refs[:chunks]
    classes_ref, _, _, products_ref, held, others_ref, scale_ref, square_ref, turned, lhs, sems = refs[chunks:]
    width, blocks = lhs.shape[1], held.shape[0] // block
    me = me_ref[0]
    fetch = fetcher(lax.div(me, chunks), block, width, classes_ref, held, others_ref, sems)

    for i in range(1, min(3, blocks)):
        for copy in fetch(i):
            copy.start()
    place(pieces, turned, me)
    lhs[...] = turned[...].T
    square_ref[...] = squares(lhs)

    def step(i, carry):
        @pl.when(i > 0)
        def _():
            for copy in fetch(i):
                copy.wait()

        @pl.when((i > 0) & (i + 2 < blocks))
        def _():
            for copy in fetch(i + 2):
                copy.start()

        rows = pl.ds(pl.multiple_of(i * block, block), block)
        products_ref[:, rows] = product(lhs[...], held[rows, :])
        total = to_lanes(squares(held, rows) + squares(others_ref, rows))
        scale_ref[:, rows] = lax.rsqrt(total + epsilon)
        return carry

    lax.fori_loop(0, blocks, step, 0)


def block_of(count, tiles):
    total = count // LANES
    while total % tiles:
        tiles -= 1
    return tiles * LANES


def near_products(me, pieces, classes):
    count, features = classes.shape
    chunks, (depth, rows) = len(pieces), pieces[0].shape
    width, block = features // 2, block_of(count, 8)
    blocks = count // block
    keep = pltpu.with_memory_space_constraint
    scalar, plain = [pl.BlockSpec(memory_space=pltpu.SMEM)], [pl.BlockSpec(memory_space=pltpu.HBM)]
    classes = keep(classes, pltpu.HBM)
    halves = VMEM((count, width), jnp.bfloat16)
    own, held, others = pl.pallas_call(
        functools.partial(load_body, chunks, block),
        out_shape=(VMEM((depth, rows), jnp.bfloat16), halves, halves),
        in_specs=scalar + plain * 2,
        out_specs=tuple(whole(3)),
        scratch_shapes=[pltpu.SemaphoreType.DMA(()), pltpu.SemaphoreType.DMA((2, 1))],
        cost_estimate=pl.CostEstimate(flops=0, bytes_accessed=2 * block * features, transcendentals=0),
        compiler_params=SMALL,
        name="load_first",
    )(me, keep(pieces[0], pltpu.HBM), classes)
    products, _, others, scale, square = pl.pallas_call(
        functools.partial(near_body, chunks, block),
        out_shape=(
            VMEM((rows, count), jnp.float32),
            halves,
            halves,
            VMEM((1, count), jnp.float32),
            VMEM((rows, LANES), jnp.float32),
        ),
        in_specs=scalar + whole(chunks) + plain + whole(2),
        out_specs=tuple(whole(5)),
        scratch_shapes=[
            VMEM((width, rows), jnp.bfloat16),
            VMEM((rows, width), jnp.bfloat16),
            pltpu.SemaphoreType.DMA((2, blocks)),
        ],
        input_output_aliases={2 + chunks: 1, 3 + chunks: 2},
        cost_estimate=pl.CostEstimate(
            flops=2 * rows * count * width, bytes_accessed=2 * count * features, transcendentals=0
        ),
        compiler_params=pltpu.CompilerParams(vmem_limit_bytes=8 << 20),
        name="near_products",
    )(me, keep(own, VMEM), *(keep(p, VMEM) for p in pieces[1:]), classes, keep(held, VMEM), keep(others, VMEM))
    return products, others, scale, square


def early_width(pieces, depth):
    return depth // 256 * 256 if pieces == 2 else 0


def early_body(early, me_ref, piece, products_ref, others_ref, square_ref, sums_ref, total_ref, lhs):
    depth, width = piece.shape[0], others_ref.shape[1]
    index = lax.rem(me_ref[0], 2)
    lhs[...] = piece[pl.ds(pl.multiple_of(index * (depth - early), 16), early), :].T
    total_ref[...] = square_ref[...] + squares(lhs)
    lanes = pl.ds(pl.multiple_of(index * (width - early), LANES), early)
    sums_ref[...] = products_ref[...] + product(lhs[...], others_ref[:, lanes])


def early_products(early, me, piece, products, others, square):
    rows, count = products.shape
    keep = pltpu.with_memory_space_constraint
    return pl.pallas_call(
        functools.partial(early_body, early),
        out_shape=(VMEM((rows, count), jnp.float32), VMEM((rows, LANES), jnp.float32)),
        in_specs=[pl.BlockSpec(memory_space=pltpu.SMEM)] + whole(4),
        out_specs=tuple(whole(2)),
        scratch_shapes=[VMEM((rows, early), jnp.bfloat16)],
        input_output_aliases={2: 0},
        cost_estimate=pl.CostEstimate(
            flops=2 * rows * count * early, bytes_accessed=8 * rows * count, transcendentals=0
        ),
        compiler_params=pltpu.CompilerParams(vmem_limit_bytes=16 << 20),
        name="early_products",
    )(me, keep(piece, VMEM), keep(products, VMEM), keep(others, VMEM), keep(square, VMEM))


def far_body(chunks, block, early, me_ref, *refs):
    pieces = refs[:chunks]
    products_ref, others_ref, scale_ref, square_ref, kernel_ref, sums_ref, turned, lhs, factor, part = refs[chunks:]
    place(pieces, turned, me_ref[0])
    start = pl.multiple_of(early - lax.rem(me_ref[0], 2) * early, LANES)
    lhs[...] = turned[pl.ds(start, lhs.shape[1]), :].T
    square = jnp.sum(square_ref[...] + squares(lhs), axis=1, keepdims=True)
    factor[...] = jnp.broadcast_to(logit_scale * lax.rsqrt(square + epsilon), factor.shape)
    part[...] = jnp.zeros_like(part)

    group = 64

    def step(i, carry):
        span = pl.ds(pl.multiple_of(i * block, block), block)
        view, scale = kernel_ref.at[:, span], scale_ref.at[:, span]
        view[...] = products_ref[:, span] + product(lhs[...], others_ref[span, pl.ds(start, lhs.shape[1])])
        for r in range(0, part.shape[0], group):
            rows = slice(r, r + group)
            total = part[rows, :]
            for at in range(0, block, LANES):
                lanes = slice(at, at + LANES)
                value = jnp.exp(view[rows, lanes] * factor[rows, :] * scale[:, lanes])
                view[rows, lanes] = value
                total = total + value
            part[rows, :] = total
        return carry

    lax.fori_loop(0, others_ref.shape[0] // block, step, 0)
    sums_ref[...] = to_lanes(part[...])


def far_kernel(early, me, pieces, products, others, scale, square):
    rows, count = products.shape
    width = others.shape[1]
    keep = pltpu.with_memory_space_constraint
    return pl.pallas_call(
        functools.partial(far_body, len(pieces), block_of(count, 20), early),
        out_shape=(VMEM((rows, count), jnp.float32), VMEM((1, rows), jnp.float32)),
        in_specs=[pl.BlockSpec(memory_space=pltpu.SMEM)] + whole(len(pieces) + 4),
        out_specs=tuple(whole(2)),
        scratch_shapes=[
            VMEM((width, rows), jnp.bfloat16),
            VMEM((rows, width - early), jnp.bfloat16),
            VMEM((rows, LANES), jnp.float32),
            VMEM((rows, LANES), jnp.float32),
        ],
        input_output_aliases={1 + len(pieces): 0},
        compiler_params=pltpu.CompilerParams(vmem_limit_bytes=16 << 20),
        name="far_kernel",
    )(me, *(keep(p, VMEM) for p in pieces), keep(products, VMEM), keep(others, VMEM), keep(scale, VMEM), keep(square, VMEM))


def added(refs):
    total = refs[0][...]
    for ref in refs[1:]:
        total = total + ref[...]
    return total


def column_body(kernel_ref, *refs):
    *sums, out_ref, spread, part, total = refs
    spread[...] = to_rows(1.0 / added(sums))
    rows, count = kernel_ref.shape
    group = 64
    part[...] = jnp.zeros_like(part)

    def chunk(i, carry):
        at = pl.ds(pl.multiple_of(i * group, group), group)
        view, scale = kernel_ref.at[at, :], spread[at, :]
        for j in range(0, count, LANES):
            lanes = slice(j, j + LANES)
            value = (view[:, lanes] * scale).reshape(group // 8, 8, LANES)
            part[:, lanes] += jnp.sum(value, axis=0)
        return carry

    lax.fori_loop(0, rows // group, chunk, 0)
    for j in range(count // LANES):
        total[j : j + 1, :] = jnp.sum(part[:, j * LANES : (j + 1) * LANES], axis=0, keepdims=True)
    out_ref[...] = jnp.broadcast_to(total[...][None], out_ref.shape)


def column_sums(kernel, sums, copies):
    rows, count = kernel.shape
    return pl.pallas_call(
        column_body,
        out_shape=VMEM((copies, count // LANES, LANES), jnp.float32),
        in_specs=whole(1 + len(sums)),
        out_specs=whole(1)[0],
        scratch_shapes=[
            VMEM((rows, LANES), jnp.float32),
            VMEM((8, count), jnp.float32),
            VMEM((count // LANES, LANES), jnp.float32),
        ],
        compiler_params=SMALL,
        name="column_sums",
    )(pltpu.with_memory_space_constraint(kernel, VMEM), *sums)


def row_body(kernel_ref, sums_ref, counts_ref, out_ref, scale_ref, part):
    scale_ref[...] = counts_ref[...].astype(jnp.float32) / jnp.sum(sums_ref[...], axis=0)
    rows, count = kernel_ref.shape
    group, block = 64, block_of(count, 8)
    part[...] = jnp.zeros_like(part)

    def chunk(j, carry):
        span = pl.ds(pl.multiple_of(j * block, block), block)
        view, scale = kernel_ref.at[:, span], scale_ref.at[pl.ds(j * (block // LANES), block // LANES), :]
        for r in range(0, rows, group):
            at = slice(r, r + group)
            total = part[at, :]
            for k in range(block // LANES):
                total = total + view[at, k * LANES : (k + 1) * LANES] * scale[k : k + 1, :]
            part[at, :] = total
        return carry

    lax.fori_loop(0, count // block, chunk, 0)
    out_ref[...] = to_lanes(part[...])


def row_sums(kernel, sums, counts, last):
    rows, _ = kernel.shape
    outputs = (VMEM((1, rows), jnp.float32), VMEM(counts.shape, jnp.float32))
    result = pl.pallas_call(
        row_body,
        out_shape=outputs[: 1 + last],
        in_specs=whole(3),
        out_specs=tuple(whole(1 + last)),
        scratch_shapes=[*outputs[1 + last :], VMEM((rows, LANES), jnp.float32)],
        compiler_params=SMALL,
        name="row_sums",
    )(pltpu.with_memory_space_constraint(kernel, VMEM), sums, counts)
    return result if last else (*result, None)


def assign_body(kernel_ref, scale_ref, *refs):
    *sums, out_ref, spread, ready, sems = refs
    spread[...] = to_rows(1.0 / added(sums))
    stripes, group, count = ready.shape

    def put(i):
        return pltpu.make_async_copy(ready.at[i], out_ref.at[pl.ds(i * group, group), :], sems.at[i])

    def step(i, carry):
        at = pl.ds(pl.multiple_of(i * group, group), group)
        for j in range(count // LANES):
            lanes = slice(j * LANES, (j + 1) * LANES)
            value = spread[at, :] * kernel_ref[at, lanes] * scale_ref[j : j + 1, :]
            ready[i, :, lanes] = value.astype(jnp.bfloat16)
        put(i).start()
        return carry

    lax.fori_loop(0, stripes, step, 0)
    for i in range(stripes):
        put(i).wait()


def assign(kernel, scale, sums):
    rows, count = kernel.shape
    group = 64
    return pl.pallas_call(
        assign_body,
        out_shape=jax.ShapeDtypeStruct((rows, count), jnp.bfloat16),
        in_specs=whole(2 + len(sums)),
        out_specs=pl.BlockSpec(memory_space=pl.ANY),
        scratch_shapes=[
            VMEM((rows, LANES), jnp.float32),
            VMEM((rows // group, group, count), jnp.bfloat16),
            pltpu.SemaphoreType.DMA((rows // group,)),
        ],
        compiler_params=SMALL,
        name="assign",
    )(pltpu.with_memory_space_constraint(kernel, VMEM), scale, *sums)


def gathered(piece, steps):
    held = [piece]
    for bit in steps:
        held = held + [exchange(h, "cls", bit) for h in held]
    return held


def shards(shapes, classes, counts):
    *low, top = bits("cls")
    me = jnp.reshape(lax.axis_index("cls"), (1,)).astype(jnp.int32)
    mine = shapes.T
    other = exchange(mine, "cls", top)
    mine_too = gathered(mine, low)
    products, others, scale, square = near_products(me, mine_too, classes)
    square, other = lax.optimization_barrier((square, other))
    pieces = gathered(other, low)
    early = early_width(len(pieces), mine.shape[0])
    if early:
        products, square = early_products(early, me, other, products, others, square)
    kernel, sums = far_kernel(early, me, pieces, products, others, scale, square)
    target = counts.reshape(-1, LANES)
    for step in range(ITERS):
        copies = column_sums(kernel, terms(sums, "cls"), lax.axis_size("shape"))
        columns = lax.all_to_all(copies, "shape", 0, 0)
        sums, col_scale = row_sums(kernel, columns, target, step == ITERS - 1)
    return assign(kernel, col_scale, terms(sums, "cls"))


def solution(mesh):
    placed = (P("shape", "cls"), P("cls", None), P("cls"))
    return jax.shard_map(
        shards, mesh=mesh, in_specs=placed, out_specs=P("shape", "cls"), check_vma=False
    )
```
